256 devices in a mesh: pair: 64 (over z, x, core), sp: 4 (over y).
Axes of the slice: x: 4, y: 4, z: 8, core: 2. Of those that a mesh axis runs over, the one named last changes fastest.
Arguments:
- gamma_pairs: bfloat16 [2, 64, 128, 30720], P(None, None, 'sp', 'pair'), may hold values from -6 to 6
- occ_coef: bfloat16 [30720, 128], P(None, 'sp'), may hold values from -0.5 to 0.5
- block_lists: int32 [4, 4, 20], replicated, may hold values from 0 to 79, as said below
- block_counts: int32 [4, 4], replicated, may hold values from 1 to 20, as said below
- block_coords: int32 [320, 2], replicated, may hold values from 0 to 239, as said below
Outputs:
- ao_gamma: bfloat16 [2, 64, 320, 128, 128], P(None, 'pair', 'sp')
The draws below stay inside these ranges and needn't reach their ends.
Inputs may be any that keep to these rules, and one draw needn't show every extreme that they name: `block_lists`: the 20 entries of one list are distinct; entries past block_counts are not used. `block_counts`: in every draw some owner gets 20 blocks from every slab. `block_coords`: every one of the 240 column blocks is the column block of some shell-pair block.
All inputs are finite; a program needn't handle non-finite values.
Results may differ from the reference program's by a relative error of at most 0.0039.
Values may be sent and summed in bfloat16 or wider, within the bound.
No kernel may reach another device: no remote copies, remote signals or barrier semaphores. Data moves between devices by JAX's collectives and lax.ppermute only.
A program may use at most 128 MiB of HBM per device.

```python
import jax
import jax.numpy as jnp
from jax import lax

BLK = 128
NBLK = 240
S_ALL = 320
OCC = 32
NBATCH = 2
OWN = 80
NAO = 30720
AUXB = 64
OCC_ALL = 128
CAPO = 20
N_SP = 4


def draw_block_lists(key, part):
    groups = S_ALL // OWN
    keys = jax.random.split(jax.random.fold_in(key, 11), groups * groups)
    chosen = jax.vmap(lambda one_key: jax.random.permutation(one_key, OWN)[:CAPO])(keys)
    return chosen.reshape(groups, groups, CAPO).astype(jnp.int32)


def draw_block_counts(key, part):
    groups = S_ALL // OWN
    counts = jax.random.randint(jax.random.fold_in(key, 21), (groups, groups), 1, CAPO + 1)
    full_owner = jax.random.randint(jax.random.fold_in(key, 22), (), 0, groups)
    owner_ids = jnp.arange(groups, dtype=jnp.int32)[None, :]
    counts = jnp.where(owner_ids == full_owner, CAPO, counts)
    return counts.astype(jnp.int32)


def draw_block_coords(key, part):
    extra = jax.random.randint(jax.random.fold_in(key, 32), (S_ALL - NBLK,), 0, NBLK)
    columns = jnp.concatenate([jnp.arange(NBLK, dtype=jnp.int32), extra.astype(jnp.int32)])
    order = jax.random.permutation(jax.random.fold_in(key, 31), S_ALL)
    col_block = columns[order]
    row_block = jax.random.randint(jax.random.fold_in(key, 33), (S_ALL,), 0, NBLK)
    return jnp.stack([row_block, col_block], axis=1).astype(jnp.int32)


def shard_levels(own_key, shape, cuts, low, top_value):
    def one(dim, shards_of):
        heights = jax.random.uniform(jax.random.fold_in(jax.random.fold_in(own_key, 6), dim), (shards_of,), jnp.float32, low / len(cuts), top_value / len(cuts))
        return jnp.repeat(jnp.exp(heights), shape[dim] // shards_of).reshape((-1,) + (1,) * (len(shape) - dim - 1))

    level = one(*cuts[0])
    for cut in cuts[1:]:
        level = level * one(*cut)
    return level


def scatter_about(rng, dims, width, reach, pieces=(), kind=jnp.bfloat16):
    factor_of = shard_levels(rng, dims, pieces, -0.22, 0.18) if pieces else 1.0
    values = jax.random.normal(rng, dims, jnp.float32) * width * factor_of
    return jnp.minimum(jnp.maximum(values, -reach), reach).astype(kind)


def setup_inputs(seed: int = 0) -> dict:
    seeds = jax.random.split(jax.random.key(seed), 6)
    return {
        "gamma_pairs": scatter_about(seeds[0], (NBATCH, AUXB, OCC_ALL, NAO), 1.0, 6.0, ((2, 4), (3, 64))),
        "occ_coef": scatter_about(seeds[1], (NAO, OCC_ALL), OCC_ALL ** -0.5, 0.5, ((1, 4),)),
        "block_lists": draw_block_lists(jax.random.fold_in(seeds[5], 71), 0),
        "block_counts": draw_block_counts(jax.random.fold_in(seeds[5], 71), 0),
        "block_coords": draw_block_coords(jax.random.fold_in(seeds[5], 71), 0),
    }


def reference(gamma_pairs, occ_coef, block_lists, block_counts, block_coords):
    slot_ids = jnp.arange(CAPO, dtype=jnp.int32)
    valid_slots = slot_ids[None, None, :] < block_counts[:, :, None]
    owned_ids = jnp.arange(OWN, dtype=jnp.int32)
    selected = (block_lists[:, :, :, None] == owned_ids[None, None, None, :]) & valid_slots[:, :, :, None]
    live_mask = jnp.any(selected, axis=2).reshape(N_SP, S_ALL).astype(jnp.float32)

    def one_block(block_index):
        row_block = block_coords[block_index, 0].astype(jnp.int32)
        col_block = block_coords[block_index, 1].astype(jnp.int32)
        coef_rows = lax.dynamic_slice_in_dim(occ_coef, row_block * BLK, BLK, 0)
        coef_rows = coef_rows.reshape(BLK, N_SP, OCC).astype(jnp.float32)
        gamma_cols = lax.dynamic_slice_in_dim(gamma_pairs, col_block * BLK, BLK, 3)
        gamma_cols = gamma_cols.reshape(NBATCH, AUXB, N_SP, OCC, BLK).astype(jnp.float32)
        products = jnp.einsum("msi,bpsin->sbpmn", coef_rows, gamma_cols)
        products = lax.optimization_barrier(products.astype(jnp.bfloat16)).astype(jnp.float32)
        totals = jnp.einsum("s,sbpmn->bpmn", live_mask[:, block_index], products)
        return totals.astype(jnp.bfloat16)

    blocks = lax.map(one_block, jnp.arange(S_ALL, dtype=jnp.int32))
    return jnp.transpose(blocks, (1, 2, 0, 3, 4))
```

```python
import functools

import jax
import jax.numpy as jnp
from jax import lax
from jax.experimental import pallas as pl
from jax.experimental.pallas import tpu as pltpu
from jax.sharding import Mesh, PartitionSpec as P

BLK = 128
NZ, NX, NCORE = 8, 4, 2
LEVELS = (11, 14, 30)
BF = jnp.bfloat16
VMEM = pl.BlockSpec(memory_space=pltpu.VMEM)
SMEM = pl.BlockSpec(memory_space=pltpu.SMEM)


def params(mib):
    return pltpu.CompilerParams(vmem_limit_bytes=mib << 20)


def cost(nbytes, flops=0):
    return pl.CostEstimate(flops=flops, bytes_accessed=nbytes, transcendentals=0)


def turn(start, k, n):
    at = start + k
    at = jnp.where(at >= n, at - n, at)
    return jnp.where(at < 0, at + n, at)


def coef_pick_kernel(me, rows, coef, *outs):
    slots = outs[0].shape[0]
    for k, out in enumerate(outs):
        base = turn(me[0], k, len(outs)) * slots

        def step(t, _):
            start = pl.multiple_of(rows[base + t] * BLK, BLK)
            out[t] = coef[:, pl.ds(start, BLK)]
            return 0

        lax.fori_loop(0, slots, step, 0, unroll=4)


def coef_pick(me, coef_t, rows, groups):
    slots, occ = rows.shape[0] // groups, coef_t.shape[0]
    return pl.pallas_call(
        coef_pick_kernel,
        out_shape=[jax.ShapeDtypeStruct((slots, occ, BLK), BF)] * groups,
        in_specs=[SMEM, SMEM, VMEM],
        out_specs=[VMEM] * groups,
        compiler_params=params(16),
        cost_estimate=cost(4 << 20),
        name="coef_pick",
    )(me, rows, coef_t)


def coef_join_kernel(me, pos, *rest):
    pieces, out, held = rest[:-2], rest[-2], rest[-1]
    groups, owned = len(pieces), out.shape[0]
    for k, piece in enumerate(pieces):
        held[turn(me[0], -k, groups)] = piece[...]

    def step(k, _):
        parts = []
        for s in range(groups):
            p = pos[s * owned + k]
            block = held[s, jnp.maximum(p, 0)]
            parts.append(jnp.where(p >= 0, block, jnp.zeros_like(block)))
        out[k] = jnp.concatenate(parts, axis=0).T
        return 0

    lax.fori_loop(0, owned, step, 0, unroll=2)


def coef_join(me, pieces, pos, owned):
    groups = len(pieces)
    slots, occ, _ = pieces[0].shape
    return pl.pallas_call(
        coef_join_kernel,
        out_shape=jax.ShapeDtypeStruct((owned, BLK, groups * occ), BF),
        in_specs=[SMEM, SMEM] + [VMEM] * groups,
        out_specs=VMEM,
        scratch_shapes=[pltpu.VMEM((groups, slots, occ, BLK), BF)],
        compiler_params=params(16),
        cost_estimate=cost(4 << 20),
        name="coef_join",
    )(me, pos, *pieces)


def plane_pick_kernel(scal, got, *rest):
    outs, tiles = rest[:-1], rest[-1]
    width = got.shape[3]
    blocks = tiles.shape[1]

    def cut(k, _):
        pz = turn(scal[0], k, NZ)
        for j in range(blocks):
            src, off = divmod(j * BLK, width)
            if off + BLK <= width:
                tiles[k, j] = got[src, pz, :, off : off + BLK]
            else:
                tiles[k, j] = jnp.concatenate(
                    [got[src, pz, :, off:width], got[src + 1, pz, :, : off + BLK - width]], axis=1
                )
        return 0

    lax.fori_loop(0, NZ, cut, 0)

    def keep(j, _):
        at = scal[1 + j]
        for k in range(NZ):
            outs[k][j] = tiles[k, at]
        return 0

    lax.fori_loop(0, outs[0].shape[0], keep, 0)


def plane_pick(got, scal, cap):
    occ = got.shape[2]
    blocks = got.shape[0] * got.shape[3] // BLK
    shape = jax.ShapeDtypeStruct((cap, occ, BLK), BF)
    return pl.pallas_call(
        plane_pick_kernel,
        out_shape=[shape] * NZ,
        in_specs=[SMEM, VMEM],
        out_specs=[VMEM] * NZ,
        scratch_shapes=[pltpu.VMEM((NZ, blocks, occ, BLK), BF)],
        compiler_params=params(20),
        cost_estimate=cost(4 << 20),
        name="plane_pick",
    )(scal, got)


def slot_pick_kernel(hop, rank, *rest):
    pieces, out, held = rest[:NZ], rest[NZ], rest[NZ + 1]
    for k in range(NZ):
        held[k] = pieces[k][...]

    def step(t, _):
        out[t] = held[hop[t], rank[t]]
        return 0

    lax.fori_loop(0, out.shape[0], step, 0, unroll=4)


def slot_pick(pieces, hop, rank):
    cap, occ, _ = pieces[0].shape
    slots = hop.shape[0]
    return pl.pallas_call(
        slot_pick_kernel,
        out_shape=jax.ShapeDtypeStruct((slots, occ, BLK), BF),
        in_specs=[SMEM, SMEM] + [VMEM] * NZ,
        out_specs=VMEM,
        scratch_shapes=[pltpu.VMEM((NZ, cap, occ, BLK), BF)],
        compiler_params=params(16),
        cost_estimate=cost(2 << 20),
        name="slot_pick",
    )(hop, rank, *pieces)


def product_kernel(per, pos, coef, gamma, *rest):
    out = rest[-1]
    groups = gamma.shape[0]
    owned = pos.shape[0] // groups
    base = pl.program_id(0) * per
    for j in range(per):
        cols = [gamma[s, jnp.maximum(pos[s * owned + base + j], 0)] for s in range(groups)]
        total = jnp.dot(
            coef[j], jnp.concatenate(cols, axis=0), preferred_element_type=jnp.float32
        )
        out[0, 0, j] = total.astype(BF)


def product(batch, batches, coef, gamma, pos, prior):
    owned = coef.shape[0]
    per = 8
    extra = [] if prior is None else [prior]
    return pl.pallas_call(
        functools.partial(product_kernel, per),
        out_shape=jax.ShapeDtypeStruct((batches, 1, owned, BLK, BLK), BF),
        grid_spec=pltpu.PrefetchScalarGridSpec(
            num_scalar_prefetch=1,
            grid=(owned // per,),
            in_specs=[
                pl.BlockSpec((per, BLK, coef.shape[2]), lambda i, pos: (i, 0, 0)),
                pl.BlockSpec(gamma.shape, lambda i, pos: (0, 0, 0, 0)),
            ]
            + [pl.BlockSpec(memory_space=pl.ANY)] * len(extra),
            out_specs=pl.BlockSpec((1, 1, per, BLK, BLK), lambda i, pos: (batch, 0, i, 0, 0)),
        ),
        input_output_aliases={3: 0} if extra else {},
        compiler_params=params(16),
        cost_estimate=cost(6 << 20, 2 * owned * BLK**3),
        name=f"product{batch}",
    )(pos, coef, gamma, *extra)


def local(gamma_pairs, occ_coef, block_lists, block_counts, block_coords):
    batches, aux, occ, width = gamma_pairs.shape
    groups = lax.axis_size("sp")
    basis = occ_coef.shape[0]
    nblk = basis // BLK
    per_plane = nblk // NZ
    plane_devs = NX * NCORE
    total_blocks = block_coords.shape[0]
    owned = total_blocks // groups
    capacity = block_lists.shape[2]
    me_s = lax.axis_index("sp")
    me_z = lax.axis_index("z")

    def exchange_plane(b):
        mine = gamma_pairs[b].reshape(NZ, plane_devs, occ, width).transpose(1, 0, 2, 3)
        return lax.all_to_all(mine, ("x", "core"), 0, 0, tiled=True)

    got0 = exchange_plane(0)

    valid = jnp.arange(capacity, dtype=jnp.int32)[None, None, :] < block_counts[:, :, None]
    lists = jnp.clip(block_lists, 0, owned - 1)
    ids = lists + (jnp.arange(groups, dtype=jnp.int32) * owned)[None, :, None]
    hit = ids.reshape(groups, -1, 1) == jnp.arange(total_blocks, dtype=jnp.int32)
    row_ids = jnp.sum(jnp.where(hit, block_coords[:, 0], 0), axis=2)
    col_ids = jnp.sum(jnp.where(hit, block_coords[:, 1], 0), axis=2)
    live_col = jnp.where(valid.reshape(groups, -1), col_ids, -1)
    need = jnp.any(live_col[:, :, None] == jnp.arange(nblk, dtype=jnp.int32), axis=1)
    need = need.reshape(groups, NZ, per_plane).astype(jnp.int32)
    most = jnp.max(jnp.sum(need, axis=2))
    my_need = lax.dynamic_index_in_dim(need, me_s, 0, keepdims=False)
    plane_ids = jnp.arange(per_plane, dtype=jnp.int32)
    before = (plane_ids[None, :] < plane_ids[:, None]).astype(jnp.int32)
    rank = jnp.sum(my_need[:, None, :] * before[None], axis=2)
    my_cols = lax.dynamic_index_in_dim(col_ids, me_s, 0, keepdims=False)
    my_rows = lax.dynamic_index_in_dim(row_ids, me_s, 0, keepdims=False)
    my_live = lax.dynamic_index_in_dim(valid.reshape(groups, -1), me_s, 0, keepdims=False)
    col_hit = my_cols[:, None] == jnp.arange(nblk, dtype=jnp.int32)
    slot_rank = jnp.sum(jnp.where(col_hit, rank.reshape(-1), 0), axis=1)
    slot_rank = jnp.where(my_live, slot_rank, 0)
    slot_hop = jnp.where(my_live, (me_z - my_cols // per_plane + NZ) % NZ, 0)
    plane_need = lax.dynamic_index_in_dim(my_need, me_z, 0, keepdims=False)
    plane_rank = lax.dynamic_index_in_dim(rank, me_z, 0, keepdims=False)
    listed = jnp.sum(
        jnp.where(
            (plane_rank[None, :] == plane_ids[:, None]) & (plane_need[None, :] > 0),
            plane_ids[None, :],
            0,
        ),
        axis=1,
    )
    scal = jnp.concatenate([me_z[None].astype(jnp.int32), listed])
    to_me = lax.dynamic_index_in_dim(lists, me_s, 1, keepdims=False)
    to_me_valid = lax.dynamic_index_in_dim(valid, me_s, 1, keepdims=False)
    at = (to_me[:, None, :] == jnp.arange(owned, dtype=jnp.int32)[None, :, None]) & to_me_valid[
        :, None, :
    ]
    slot_no = jnp.arange(capacity, dtype=jnp.int32) + 1
    pos = (jnp.sum(jnp.where(at, slot_no, 0), axis=2) - 1).reshape(-1)

    me = me_s[None].astype(jnp.int32)
    sent = coef_pick(me, occ_coef.T, my_rows, groups)
    pieces = [sent[0]]
    for k in range(1, groups):
        pieces.append(lax.ppermute(sent[k], "sp", [(i, (i + k) % groups) for i in range(groups)]))
    coef = coef_join(me, pieces, pos, owned)

    def finish(cap, got0, coef, pos, scal, slot_hop, slot_rank):
        out = None
        got = got0
        for b in range(batches):
            picked = plane_pick(got, scal, cap)
            pieces = [picked[0]]
            for k in range(1, NZ):
                pieces.append(
                    lax.ppermute(picked[k], "z", [(i, (i + k) % NZ) for i in range(NZ)])
                )
            if b + 1 < batches:
                got = exchange_plane(b + 1)
            send = slot_pick(pieces, slot_hop, slot_rank).reshape(groups, capacity, occ, BLK)
            gamma = lax.all_to_all(send, "sp", 0, 0, tiled=True)
            out = product(b, batches, coef, gamma, pos, out)
        return out

    level = jnp.sum((most > jnp.array(LEVELS[:-1], jnp.int32)).astype(jnp.int32))
    return lax.switch(
        level,
        [functools.partial(finish, cap) for cap in LEVELS],
        got0,
        coef,
        pos,
        scal,
        slot_hop,
        slot_rank,
    )


def solution(mesh):
    groups = mesh.shape["sp"]
    grid = Mesh(mesh.devices.reshape(NZ, NX, NCORE, groups), ("z", "x", "core", "sp"))
    pair = ("z", "x", "core")
    in_specs = (P(None, None, "sp", pair), P(None, "sp"), P(), P(), P())
    out_specs = P(None, pair, "sp", None, None)
    return jax.shard_map(local, mesh=grid, in_specs=in_specs, out_specs=out_specs, check_vma=False)
```

```python
import functools

import jax
import jax.numpy as jnp
from jax import lax
from jax.experimental import pallas as pl
from jax.experimental.pallas import tpu as pltpu
from jax.sharding import Mesh, PartitionSpec as P

BLK = 128
NZ, NX, NCORE = 8, 4, 2
LEVELS = (13, 30)
BF = jnp.bfloat16
VMEM = pl.BlockSpec(memory_space=pltpu.VMEM)
ANY = pl.BlockSpec(memory_space=pl.ANY)
SMEM = pl.BlockSpec(memory_space=pltpu.SMEM)


def params(mib):
    return pltpu.CompilerParams(vmem_limit_bytes=mib << 20)


def cost(nbytes, flops=0):
    return pl.CostEstimate(flops=flops, bytes_accessed=nbytes, transcendentals=0)


def turn(start, k, n):
    at = start + k
    at = jnp.where(at >= n, at - n, at)
    return jnp.where(at < 0, at + n, at)


def coef_pick_kernel(me, rows, coef, after, *outs):
    slots = outs[0].shape[0]
    for k, out in enumerate(outs):
        base = turn(me[0], k, len(outs)) * slots

        def step(t, _):
            start = pl.multiple_of(rows[base + t] * BLK, BLK)
            out[t] = coef[:, pl.ds(start, BLK)]
            return 0

        lax.fori_loop(0, slots, step, 0, unroll=4)


def coef_pick(me, coef_t, rows, after, groups):
    slots, occ = rows.shape[0] // groups, coef_t.shape[0]
    return pl.pallas_call(
        coef_pick_kernel,
        out_shape=[jax.ShapeDtypeStruct((slots, occ, BLK), BF)] * groups,
        in_specs=[SMEM, SMEM, VMEM, ANY],
        out_specs=[VMEM] * groups,
        compiler_params=params(16),
        cost_estimate=cost(4 << 20),
        name="coef_pick",
    )(me, rows, coef_t, after)


def coef_join_kernel(me, pos, *rest):
    pieces, out, held = rest[:-2], rest[-2], rest[-1]
    groups, owned = len(pieces), out.shape[0]
    for k, piece in enumerate(pieces):
        held[turn(me[0], -k, groups)] = piece[...]

    def step(k, _):
        parts = []
        for s in range(groups):
            p = pos[s * owned + k]
            block = held[s, jnp.maximum(p, 0)]
            parts.append(jnp.where(p >= 0, block, jnp.zeros_like(block)))
        out[k] = jnp.concatenate(parts, axis=0).T
        return 0

    lax.fori_loop(0, owned, step, 0, unroll=2)


def coef_join(me, pieces, pos, owned):
    groups = len(pieces)
    slots, occ, _ = pieces[0].shape
    return pl.pallas_call(
        coef_join_kernel,
        out_shape=jax.ShapeDtypeStruct((owned, BLK, groups * occ), BF),
        in_specs=[SMEM, SMEM] + [VMEM] * groups,
        out_specs=VMEM,
        scratch_shapes=[pltpu.VMEM((groups, slots, occ, BLK), BF)],
        compiler_params=params(16),
        cost_estimate=cost(4 << 20),
        name="coef_join",
    )(me, pos, *pieces)


def plane_split_kernel(batch, at, pairs, *rest):
    outs, sems = rest[:-1], rest[-1]
    copies = []
    for k, out in enumerate(outs):
        px = turn(at[0], k // NCORE, NX)
        pc = at[1] if k % NCORE == 0 else 1 - at[1]
        copies.append(pltpu.make_async_copy(pairs.at[batch, :, px, pc], out, sems.at[k]))
    for copy in copies:
        copy.start()
    for copy in copies:
        copy.wait()


def plane_split(batch, at, pairs):
    _, nz, nx, nc, occ, width = pairs.shape
    return pl.pallas_call(
        functools.partial(plane_split_kernel, batch),
        out_shape=[jax.ShapeDtypeStruct((nz, occ, width), BF)] * (nx * nc),
        in_specs=[SMEM, pl.BlockSpec(memory_space=pltpu.HBM)],
        out_specs=[VMEM] * (nx * nc),
        scratch_shapes=[pltpu.SemaphoreType.DMA((nx * nc,))],
        compiler_params=params(60),
        cost_estimate=cost(4 << 20),
        name=f"plane_split{batch}",
    )(at, pairs)


def plane_pick_kernel(at, listed, *rest):
    pieces, (out, got, tiles) = rest[:-3], rest[-3:]
    width = got.shape[3]
    blocks = tiles.shape[1]
    for k, piece in enumerate(pieces):
        sx = turn(at[0], -(k // NCORE), NX)
        sc = at[1] if k % NCORE == 0 else 1 - at[1]
        got[sx * NCORE + sc] = piece[...]

    def cut(pz, _):
        for j in range(blocks):
            src, off = divmod(j * BLK, width)
            if off + BLK <= width:
                tiles[pz, j] = got[src, pz, :, off : off + BLK]
            else:
                tiles[pz, j] = jnp.concatenate(
                    [got[src, pz, :, off:width], got[src + 1, pz, :, : off + BLK - width]], axis=1
                )
        return 0

    lax.fori_loop(0, NZ, cut, 0)

    def keep(j, _):
        block = listed[j]
        for pz in range(NZ):
            out[pz, j] = tiles[pz, block]
        return 0

    lax.fori_loop(0, out.shape[1], keep, 0)


def plane_pick(at, listed, pieces, cap):
    nz, occ, width = pieces[0].shape
    n = len(pieces)
    return pl.pallas_call(
        plane_pick_kernel,
        out_shape=jax.ShapeDtypeStruct((nz, cap, occ, BLK), BF),
        in_specs=[SMEM, SMEM] + [VMEM] * n,
        out_specs=VMEM,
        scratch_shapes=[
            pltpu.VMEM((n, nz, occ, width), BF),
            pltpu.VMEM((nz, n * width // BLK, occ, BLK), BF),
        ],
        compiler_params=params(24),
        cost_estimate=cost(4 << 20),
        name="plane_pick",
    )(at, listed, *pieces)


def slot_pick_kernel(me, plane, rank, got, *outs):
    slots = outs[0].shape[0]
    for k, out in enumerate(outs):
        base = turn(me[0], k, len(outs)) * slots

        def step(t, _):
            out[t] = got[plane[base + t], rank[base + t]]
            return 0

        lax.fori_loop(0, slots, step, 0, unroll=4)


def slot_pick(me, plane, rank, got, groups):
    slots = plane.shape[0] // groups
    occ = got.shape[2]
    return pl.pallas_call(
        slot_pick_kernel,
        out_shape=[jax.ShapeDtypeStruct((slots, occ, BLK), BF)] * groups,
        in_specs=[SMEM, SMEM, SMEM, VMEM],
        out_specs=[VMEM] * groups,
        compiler_params=params(16),
        cost_estimate=cost(2 << 20),
        name="slot_pick",
    )(me, plane, rank, got)


def product_kernel(per, groups, me, pos, coef, *rest):
    gamma, (out, held) = rest[:groups], rest[-2:]
    owned = pos.shape[0] // groups
    step = pl.program_id(0)

    @pl.when(step == 0)
    def _():
        for k in range(groups):
            held[turn(me[0], -k, groups)] = gamma[k][...]

    for j in range(per):
        at = [jnp.maximum(pos[s * owned + step * per + j], 0) for s in range(groups)]
        cols = jnp.concatenate([held[s, at[s]] for s in range(groups)], axis=0)
        total = jnp.dot(coef[j], cols, preferred_element_type=jnp.float32)
        out[0, 0, j] = total.astype(BF)


def product(batch, batches, me, coef, gamma, pos, prior):
    owned = coef.shape[0]
    groups = len(gamma)
    per = 20
    extra = [] if prior is None else [prior]
    return pl.pallas_call(
        functools.partial(product_kernel, per, groups),
        out_shape=jax.ShapeDtypeStruct((batches, 1, owned, BLK, BLK), BF),
        grid_spec=pltpu.PrefetchScalarGridSpec(
            num_scalar_prefetch=2,
            grid=(owned // per,),
            in_specs=[pl.BlockSpec((per, BLK, coef.shape[2]), lambda i, *_: (i, 0, 0))]
            + [pl.BlockSpec(gamma[0].shape, lambda i, *_: (0, 0, 0))] * groups
            + [ANY] * len(extra),
            out_specs=pl.BlockSpec((1, 1, per, BLK, BLK), lambda i, *_: (batch, 0, i, 0, 0)),
            scratch_shapes=[pltpu.VMEM((groups,) + gamma[0].shape, BF)],
        ),
        input_output_aliases={3 + groups: 0} if extra else {},
        compiler_params=params(16),
        cost_estimate=cost(6 << 20, 2 * owned * BLK**3),
        name=f"product{batch}",
    )(me, pos, coef, *gamma, *extra)


def local(gamma_pairs, occ_coef, block_lists, block_counts, block_coords):
    batches, aux, occ, width = gamma_pairs.shape
    groups = lax.axis_size("sp")
    basis = occ_coef.shape[0]
    nblk = basis // BLK
    per_plane = nblk // NZ
    plane_devs = NX * NCORE
    total_blocks = block_coords.shape[0]
    owned = total_blocks // groups
    capacity = block_lists.shape[2]
    me_s = lax.axis_index("sp")
    me_z = lax.axis_index("z")

    at = jnp.stack([lax.axis_index("x"), lax.axis_index("core")]).astype(jnp.int32)
    pairs = gamma_pairs.reshape(batches, NZ, NX, NCORE, occ, width)

    def exchange_plane(split):
        got = [split[0]]
        for k in range(1, plane_devs):
            dx, dc = divmod(k, NCORE)
            moves = [
                (x * NCORE + c, (x + dx) % NX * NCORE + (c ^ dc))
                for x in range(NX)
                for c in range(NCORE)
            ]
            got.append(lax.ppermute(split[k], ("x", "core"), moves))
        return got

    got0 = exchange_plane(plane_split(0, at, pairs))
    split1 = plane_split(1, at, pairs)

    valid = jnp.arange(capacity, dtype=jnp.int32)[None, None, :] < block_counts[:, :, None]
    lists = jnp.clip(block_lists, 0, owned - 1)
    ids = lists + (jnp.arange(groups, dtype=jnp.int32) * owned)[None, :, None]
    hit = ids.reshape(groups, -1, 1) == jnp.arange(total_blocks, dtype=jnp.int32)
    row_ids = jnp.sum(jnp.where(hit, block_coords[:, 0], 0), axis=2)
    col_ids = jnp.sum(jnp.where(hit, block_coords[:, 1], 0), axis=2)
    live_col = jnp.where(valid.reshape(groups, -1), col_ids, -1)
    need = jnp.any(live_col[:, :, None] == jnp.arange(nblk, dtype=jnp.int32), axis=1)
    need = need.reshape(groups, NZ, per_plane).astype(jnp.int32)
    most = jnp.max(jnp.sum(need, axis=2))
    my_need = lax.dynamic_index_in_dim(need, me_s, 0, keepdims=False)
    plane_ids = jnp.arange(per_plane, dtype=jnp.int32)
    before = (plane_ids[None, :] < plane_ids[:, None]).astype(jnp.int32)
    rank = jnp.sum(my_need[:, None, :] * before[None], axis=2)
    my_cols = lax.dynamic_index_in_dim(col_ids, me_s, 0, keepdims=False)
    my_rows = lax.dynamic_index_in_dim(row_ids, me_s, 0, keepdims=False)
    my_live = lax.dynamic_index_in_dim(valid.reshape(groups, -1), me_s, 0, keepdims=False)
    col_hit = my_cols[:, None] == jnp.arange(nblk, dtype=jnp.int32)
    slot_rank = jnp.sum(jnp.where(col_hit, rank.reshape(-1), 0), axis=1)
    slot_rank = jnp.where(my_live, slot_rank, 0)
    slot_plane = jnp.where(my_live, my_cols // per_plane, 0)
    plane_need = lax.dynamic_index_in_dim(my_need, me_z, 0, keepdims=False)
    plane_rank = lax.dynamic_index_in_dim(rank, me_z, 0, keepdims=False)
    listed = jnp.sum(
        jnp.where(
            (plane_rank[None, :] == plane_ids[:, None]) & (plane_need[None, :] > 0),
            plane_ids[None, :],
            0,
        ),
        axis=1,
    )
    to_me = lax.dynamic_index_in_dim(lists, me_s, 1, keepdims=False)
    to_me_valid = lax.dynamic_index_in_dim(valid, me_s, 1, keepdims=False)
    hits = (to_me[:, None, :] == jnp.arange(owned, dtype=jnp.int32)[None, :, None]) & to_me_valid[
        :, None, :
    ]
    slot_no = jnp.arange(capacity, dtype=jnp.int32) + 1
    pos = (jnp.sum(jnp.where(hits, slot_no, 0), axis=2) - 1).reshape(-1)

    me = me_s[None].astype(jnp.int32)
    def exchange_owners(sent):
        return [sent[0]] + [
            lax.ppermute(sent[k], "sp", [(i, (i + k) % groups) for i in range(groups)])
            for k in range(1, groups)
        ]

    def finish(cap, got0, split1, coef_t, my_rows, pos, listed, slot_plane, slot_rank):
        def planes(got):
            return lax.all_to_all(plane_pick(at, listed, got, cap), "z", 0, 0, tiled=True)

        def owners(got):
            return exchange_owners(slot_pick(me, slot_plane, slot_rank, got, groups))

        held0 = planes(got0)
        got1 = exchange_plane(split1)
        coef_parts = exchange_owners(coef_pick(me, coef_t, my_rows, got1[1], groups))
        coef = coef_join(me, coef_parts, pos, owned)
        held1 = planes(got1)
        out = product(0, batches, me, coef, owners(held0), pos, None)
        return product(1, batches, me, coef, owners(held1), pos, out)

    level = jnp.sum((most > jnp.array(LEVELS[:-1], jnp.int32)).astype(jnp.int32))
    level, my_rows, pos, listed, slot_plane, slot_rank = lax.optimization_barrier(
        (level, my_rows, pos, listed, slot_plane, slot_rank)
    )
    return lax.switch(
        level,
        [functools.partial(finish, cap) for cap in LEVELS],
        got0,
        split1,
        occ_coef.T,
        my_rows,
        pos,
        listed,
        slot_plane,
        slot_rank,
    )


def solution(mesh):
    groups = mesh.shape["sp"]
    grid = Mesh(mesh.devices.reshape(NZ, NX, NCORE, groups), ("z", "x", "core", "sp"))
    pair = ("z", "x", "core")
    in_specs = (P(None, None, "sp", pair), P(None, "sp"), P(), P(), P())
    out_specs = P(None, pair, "sp", None, None)
    return jax.shard_map(local, mesh=grid, in_specs=in_specs, out_specs=out_specs, check_vma=False)
```

```python
import functools

import jax
import jax.numpy as jnp
from jax import lax
from jax.experimental import pallas as pl
from jax.experimental.pallas import tpu as pltpu
from jax.sharding import Mesh, PartitionSpec as P

BLK = 128
NZ, NX, NCORE = 8, 4, 2
CAP = 13
AFTER = 5
BF = jnp.bfloat16
VMEM = pl.BlockSpec(memory_space=pltpu.VMEM)
ANY = pl.BlockSpec(memory_space=pl.ANY)
SMEM = pl.BlockSpec(memory_space=pltpu.SMEM)


def params(mib):
    return pltpu.CompilerParams(vmem_limit_bytes=mib << 20)


def cost(nbytes, flops=0):
    return pl.CostEstimate(flops=flops, bytes_accessed=nbytes, transcendentals=0)


def turn(start, k, n):
    at = start + k
    at = jnp.where(at >= n, at - n, at)
    return jnp.where(at < 0, at + n, at)


def coef_pick_kernel(me, rows, coef, after, *outs):
    slots = outs[0].shape[0]
    for k, out in enumerate(outs):
        base = turn(me[0], k, len(outs)) * slots

        def step(t, _):
            start = pl.multiple_of(rows[base + t] * BLK, BLK)
            out[t] = coef[:, pl.ds(start, BLK)]
            return 0

        lax.fori_loop(0, slots, step, 0, unroll=4)


def coef_pick(me, coef_t, rows, after, groups):
    slots, occ = rows.shape[0] // groups, coef_t.shape[0]
    return pl.pallas_call(
        coef_pick_kernel,
        out_shape=[jax.ShapeDtypeStruct((slots, occ, BLK), BF)] * groups,
        in_specs=[SMEM, SMEM, VMEM, ANY],
        out_specs=[VMEM] * groups,
        compiler_params=params(16),
        cost_estimate=cost(4 << 20),
        name="coef_pick",
    )(me, rows, coef_t, after)


def coef_join_kernel(me, pos, *rest):
    pieces, out, held = rest[:-2], rest[-2], rest[-1]
    groups, owned = len(pieces), out.shape[0]
    for k, piece in enumerate(pieces):
        held[turn(me[0], -k, groups)] = piece[...]

    def step(k, _):
        parts = []
        for s in range(groups):
            p = pos[s * owned + k]
            block = held[s, jnp.maximum(p, 0)]
            parts.append(jnp.where(p >= 0, block, jnp.zeros_like(block)))
        out[k] = jnp.concatenate(parts, axis=0).T
        return 0

    lax.fori_loop(0, owned, step, 0, unroll=2)


def coef_join(me, pieces, pos, owned):
    groups = len(pieces)
    slots, occ, _ = pieces[0].shape
    return pl.pallas_call(
        coef_join_kernel,
        out_shape=jax.ShapeDtypeStruct((owned, BLK, groups * occ), BF),
        in_specs=[SMEM, SMEM] + [VMEM] * groups,
        out_specs=VMEM,
        scratch_shapes=[pltpu.VMEM((groups, slots, occ, BLK), BF)],
        compiler_params=params(16),
        cost_estimate=cost(4 << 20),
        name="coef_join",
    )(me, pos, *pieces)


def plane_split_kernel(batch, at, pairs, *rest):
    outs, sems = rest[:-1], rest[-1]
    copies = []
    for k, out in enumerate(outs):
        px = turn(at[0], k // NCORE, NX)
        pc = at[1] if k % NCORE == 0 else 1 - at[1]
        copies.append(pltpu.make_async_copy(pairs.at[batch, :, px, pc], out, sems.at[k]))
    for copy in copies:
        copy.start()
    for copy in copies:
        copy.wait()


def plane_split(batch, at, pairs):
    _, nz, nx, nc, occ, width = pairs.shape
    return pl.pallas_call(
        functools.partial(plane_split_kernel, batch),
        out_shape=[jax.ShapeDtypeStruct((nz, occ, width), BF)] * (nx * nc),
        in_specs=[SMEM, pl.BlockSpec(memory_space=pltpu.HBM)],
        out_specs=[VMEM] * (nx * nc),
        scratch_shapes=[pltpu.SemaphoreType.DMA((nx * nc,))],
        compiler_params=params(8),
        cost_estimate=cost(4 << 20),
        name=f"plane_split{batch}",
    )(at, pairs)


def plane_pack_kernel(batch, pairs, *rest):
    out, sems = rest[-2:]
    copies = [
        pltpu.make_async_copy(pairs.at[batch, :, k // NCORE, k % NCORE], out.at[k], sems.at[k])
        for k in range(NX * NCORE)
    ]
    for copy in copies:
        copy.start()
    for copy in copies:
        copy.wait()


def plane_pack(batch, pairs, after):
    _, nz, nx, nc, occ, width = pairs.shape
    return pl.pallas_call(
        functools.partial(plane_pack_kernel, batch),
        out_shape=jax.ShapeDtypeStruct((nx * nc, nz, occ, width), BF),
        in_specs=[pl.BlockSpec(memory_space=pltpu.HBM)] + [ANY] * len(after),
        out_specs=VMEM,
        scratch_shapes=[pltpu.SemaphoreType.DMA((nx * nc,))],
        compiler_params=params(8),
        cost_estimate=cost(4 << 20),
        name="plane_pack",
    )(pairs, *after)


def listed_tiles(out_of, count, listed, got, tiles):
    width = got.shape[3]
    blocks = tiles.shape[1]

    def cut(pz, _):
        for j in range(blocks):
            src, off = divmod(j * BLK, width)
            if off + BLK <= width:
                tiles[pz, j] = got[src, pz, :, off : off + BLK]
            else:
                tiles[pz, j] = jnp.concatenate(
                    [got[src, pz, :, off:width], got[src + 1, pz, :, : off + BLK - width]], axis=1
                )
        return 0

    lax.fori_loop(0, NZ, cut, 0)

    def keep(j, _):
        block = listed[j]
        for k in range(NZ):
            out_of(k, j, block)
        return 0

    lax.fori_loop(0, count, keep, 0)


def plane_pick_turned_kernel(at, listed, *rest):
    pieces, outs, (got, tiles) = rest[: NX * NCORE], rest[NX * NCORE : -2], rest[-2:]
    for k, piece in enumerate(pieces):
        sx = turn(at[0], -(k // NCORE), NX)
        sc = at[1] if k % NCORE == 0 else 1 - at[1]
        got[sx * NCORE + sc] = piece[...]

    def put(k, j, block):
        outs[k][j] = tiles[turn(at[2], k, NZ), block]

    listed_tiles(put, outs[0].shape[0], listed, got, tiles)


def plane_pick_turned(at, listed, pieces, cap):
    nz, occ, width = pieces[0].shape
    n = len(pieces)
    return pl.pallas_call(
        plane_pick_turned_kernel,
        out_shape=[jax.ShapeDtypeStruct((cap, occ, BLK), BF)] * nz,
        in_specs=[SMEM, SMEM] + [VMEM] * n,
        out_specs=[VMEM] * nz,
        scratch_shapes=[
            pltpu.VMEM((n, nz, occ, width), BF),
            pltpu.VMEM((nz, n * width // BLK, occ, BLK), BF),
        ],
        compiler_params=params(24),
        cost_estimate=cost(4 << 20),
        name="plane_pick_turned",
    )(at, listed, *pieces)


def plane_pick_kernel(listed, got, after, out, tiles):
    def put(k, j, block):
        out[k, j] = tiles[k, block]

    listed_tiles(put, out.shape[1], listed, got, tiles)


def plane_pick(listed, got, cap, after):
    n, nz, occ, width = got.shape
    return pl.pallas_call(
        plane_pick_kernel,
        out_shape=jax.ShapeDtypeStruct((nz, cap, occ, BLK), BF),
        in_specs=[SMEM, VMEM, ANY],
        out_specs=VMEM,
        scratch_shapes=[pltpu.VMEM((nz, n * width // BLK, occ, BLK), BF)],
        compiler_params=params(20),
        cost_estimate=cost(4 << 20),
        name="plane_pick",
    )(listed, got, after)


def slot_pick_kernel(me, plane, rank, after, *rest):
    if len(rest) <= NZ:
        got, outs = rest[0], rest[1:]
    else:
        pieces, outs, got = rest[:NZ], rest[NZ:-1], rest[-1]
        for k, piece in enumerate(pieces):
            got[turn(me[1], -k, NZ)] = piece[...]
    slots = outs[0].shape[0]
    for k, out in enumerate(outs):
        base = turn(me[0], k, len(outs)) * slots

        def step(t, _):
            out[t] = got[plane[base + t], rank[base + t]]
            return 0

        lax.fori_loop(0, slots, step, 0, unroll=4)


def slot_pick(me, plane, rank, got, after, groups):
    pieces = got if isinstance(got, list) else [got]
    slots = plane.shape[0] // groups
    cap, occ, _ = pieces[0].shape[-3:]
    turned = len(pieces) > 1
    return pl.pallas_call(
        slot_pick_kernel,
        out_shape=[jax.ShapeDtypeStruct((slots, occ, BLK), BF)] * groups,
        in_specs=[SMEM, SMEM, SMEM, ANY] + [VMEM] * len(pieces),
        out_specs=[VMEM] * groups,
        scratch_shapes=[pltpu.VMEM((NZ, cap, occ, BLK), BF)] if turned else [],
        compiler_params=params(16),
        cost_estimate=cost(2 << 20),
        name="slot_pick",
    )(me, plane, rank, after, *pieces)


def product_kernel(per, groups, me, pos, coef, *rest):
    gamma, (out, held) = rest[:groups], rest[-2:]
    owned = pos.shape[0] // groups
    step = pl.program_id(0)

    @pl.when(step == 0)
    def _():
        for k in range(groups):
            held[turn(me[0], -k, groups)] = gamma[k][...]

    for j in range(per):
        at = [jnp.maximum(pos[s * owned + step * per + j], 0) for s in range(groups)]
        cols = jnp.concatenate([held[s, at[s]] for s in range(groups)], axis=0)
        total = jnp.dot(coef[j], cols, preferred_element_type=jnp.float32)
        out[0, 0, j] = total.astype(BF)


def product(batch, batches, me, coef, gamma, pos, prior):
    owned = coef.shape[0]
    groups = len(gamma)
    per = 20
    extra = [] if prior is None else [prior]
    return pl.pallas_call(
        functools.partial(product_kernel, per, groups),
        out_shape=jax.ShapeDtypeStruct((batches, 1, owned, BLK, BLK), BF),
        grid_spec=pltpu.PrefetchScalarGridSpec(
            num_scalar_prefetch=2,
            grid=(owned // per,),
            in_specs=[pl.BlockSpec((per, BLK, coef.shape[2]), lambda i, *_: (i, 0, 0))]
            + [pl.BlockSpec(gamma[0].shape, lambda i, *_: (0, 0, 0))] * groups
            + [ANY] * len(extra),
            out_specs=pl.BlockSpec((1, 1, per, BLK, BLK), lambda i, *_: (batch, 0, i, 0, 0)),
            scratch_shapes=[pltpu.VMEM((groups,) + gamma[0].shape, BF)],
        ),
        input_output_aliases={3 + groups: 0} if extra else {},
        compiler_params=params(16),
        cost_estimate=cost(6 << 20, 2 * owned * BLK**3),
        name=f"product{batch}",
    )(me, pos, coef, *gamma, *extra)


def local(gamma_pairs, occ_coef, block_lists, block_counts, block_coords):
    batches, aux, occ, width = gamma_pairs.shape
    groups = lax.axis_size("sp")
    basis = occ_coef.shape[0]
    nblk = basis // BLK
    per_plane = nblk // NZ
    plane_devs = NX * NCORE
    total_blocks = block_coords.shape[0]
    owned = total_blocks // groups
    capacity = block_lists.shape[2]
    me_s = lax.axis_index("sp")
    me_z = lax.axis_index("z")

    at = jnp.stack([lax.axis_index(name) for name in ("x", "core", "z")]).astype(jnp.int32)
    pairs = gamma_pairs.reshape(batches, NZ, NX, NCORE, occ, width)
    pairs = pltpu.with_memory_space_constraint(pairs, pltpu.HBM)

    def exchange_plane(split):
        got = [split[0]]
        for k in range(1, plane_devs):
            dx, dc = divmod(k, NCORE)
            moves = [
                (x * NCORE + c, (x + dx) % NX * NCORE + (c ^ dc))
                for x in range(NX)
                for c in range(NCORE)
            ]
            got.append(lax.ppermute(split[k], ("x", "core"), moves))
        return got

    got0 = exchange_plane(plane_split(0, at, pairs))
    got1 = lax.all_to_all(plane_pack(1, pairs, got0[1 : 1 + AFTER]), ("x", "core"), 0, 0, tiled=True)

    valid = jnp.arange(capacity, dtype=jnp.int32)[None, None, :] < block_counts[:, :, None]
    lists = jnp.clip(block_lists, 0, owned - 1)
    ids = lists + (jnp.arange(groups, dtype=jnp.int32) * owned)[None, :, None]
    hit = ids.reshape(groups, -1, 1) == jnp.arange(total_blocks, dtype=jnp.int32)
    row_ids = jnp.sum(jnp.where(hit, block_coords[:, 0], 0), axis=2)
    col_ids = jnp.sum(jnp.where(hit, block_coords[:, 1], 0), axis=2)
    live_col = jnp.where(valid.reshape(groups, -1), col_ids, -1)
    need = jnp.any(live_col[:, :, None] == jnp.arange(nblk, dtype=jnp.int32), axis=1)
    need = need.reshape(groups, NZ, per_plane).astype(jnp.int32)
    most = jnp.max(jnp.sum(need, axis=2))
    my_need = lax.dynamic_index_in_dim(need, me_s, 0, keepdims=False)
    plane_ids = jnp.arange(per_plane, dtype=jnp.int32)
    before = (plane_ids[None, :] < plane_ids[:, None]).astype(jnp.int32)
    rank = jnp.sum(my_need[:, None, :] * before[None], axis=2)
    my_cols = lax.dynamic_index_in_dim(col_ids, me_s, 0, keepdims=False)
    my_rows = lax.dynamic_index_in_dim(row_ids, me_s, 0, keepdims=False)
    my_live = lax.dynamic_index_in_dim(valid.reshape(groups, -1), me_s, 0, keepdims=False)
    col_hit = my_cols[:, None] == jnp.arange(nblk, dtype=jnp.int32)
    slot_rank = jnp.sum(jnp.where(col_hit, rank.reshape(-1), 0), axis=1)
    slot_rank = jnp.where(my_live, slot_rank, 0)
    slot_plane = jnp.where(my_live, my_cols // per_plane, 0)
    plane_need = lax.dynamic_index_in_dim(my_need, me_z, 0, keepdims=False)
    plane_rank = lax.dynamic_index_in_dim(rank, me_z, 0, keepdims=False)
    listed = jnp.sum(
        jnp.where(
            (plane_rank[None, :] == plane_ids[:, None]) & (plane_need[None, :] > 0),
            plane_ids[None, :],
            0,
        ),
        axis=1,
    )
    to_me = lax.dynamic_index_in_dim(lists, me_s, 1, keepdims=False)
    to_me_valid = lax.dynamic_index_in_dim(valid, me_s, 1, keepdims=False)
    hits = (to_me[:, None, :] == jnp.arange(owned, dtype=jnp.int32)[None, :, None]) & to_me_valid[
        :, None, :
    ]
    slot_no = jnp.arange(capacity, dtype=jnp.int32) + 1
    pos = (jnp.sum(jnp.where(hits, slot_no, 0), axis=2) - 1).reshape(-1)

    me = jnp.stack([me_s, me_z]).astype(jnp.int32)
    def exchange_owners(sent):
        return [sent[0]] + [
            lax.ppermute(sent[k], "sp", [(i, (i + k) % groups) for i in range(groups)])
            for k in range(1, groups)
        ]

    listed = listed[:CAP]
    slot_at = jnp.minimum(slot_rank, CAP - 1)

    sent0 = plane_pick_turned(at, listed, got0, CAP)
    held0 = [sent0[0]] + [
        lax.ppermute(sent0[k], "z", [(i, (i + k) % NZ) for i in range(NZ)]) for k in range(1, NZ)
    ]
    parts0 = slot_pick(me, slot_plane, slot_at, held0, me, groups)
    coef_parts = exchange_owners(coef_pick(me, occ_coef.T, my_rows, parts0[0], groups))
    coef = coef_join(me, coef_parts, pos, owned)
    held1 = lax.all_to_all(plane_pick(listed, got1, CAP, parts0[0]), "z", 0, 0, tiled=True)
    out = product(0, batches, me, coef, exchange_owners(parts0), pos, None)
    parts1 = slot_pick(me, slot_plane, slot_at, held1, out[0, 0, 0, :8], groups)
    out = product(1, batches, me, coef, exchange_owners(parts1), pos, out)

    def all_columns(out):
        gathered = lax.all_to_all(gamma_pairs, ("z", "x", "core"), 1, 3, tiled=True)
        blocks = gathered.reshape(batches, occ, nblk, BLK)
        taken = jnp.take(blocks, my_cols, axis=2).transpose(0, 2, 1, 3)
        for b in range(batches):
            sent = taken[b].reshape(groups, capacity, occ, BLK)
            gamma = lax.all_to_all(sent, "sp", 0, 0, tiled=True)
            parts = [
                lax.dynamic_index_in_dim(gamma, (me_s - k + groups) % groups, 0, keepdims=False)
                for k in range(groups)
            ]
            out = product(b, batches, me, coef, parts, pos, out)
        return out

    return lax.cond(most > CAP, all_columns, lambda out: out, out)


def solution(mesh):
    groups = mesh.shape["sp"]
    grid = Mesh(mesh.devices.reshape(NZ, NX, NCORE, groups), ("z", "x", "core", "sp"))
    pair = ("z", "x", "core")
    in_specs = (P(None, None, "sp", pair), P(None, "sp"), P(), P(), P())
    out_specs = P(None, pair, "sp", None, None)
    return jax.shard_map(local, mesh=grid, in_specs=in_specs, out_specs=out_specs, check_vma=False)
```

```python
import functools

import jax
import jax.numpy as jnp
from jax import lax
from jax.experimental import pallas as pl
from jax.experimental.pallas import tpu as pltpu
from jax.sharding import Mesh, PartitionSpec as P

BLK = 128
NZ, NX, NCORE = 8, 4, 2
CAP = 13
BF = jnp.bfloat16
VMEM = pl.BlockSpec(memory_space=pltpu.VMEM)
ANY = pl.BlockSpec(memory_space=pl.ANY)
SMEM = pl.BlockSpec(memory_space=pltpu.SMEM)


def params(mib):
    return pltpu.CompilerParams(vmem_limit_bytes=mib << 20)


def cost(nbytes, flops=0):
    return pl.CostEstimate(flops=flops, bytes_accessed=nbytes, transcendentals=0)


def turn(start, k, n):
    at = start + k
    at = jnp.where(at >= n, at - n, at)
    return jnp.where(at < 0, at + n, at)


def coef_pick_kernel(me, rows, coef, after, *outs):
    slots = outs[0].shape[0]
    for k, out in enumerate(outs):
        base = turn(me[0], k, len(outs)) * slots

        def step(t, _):
            start = pl.multiple_of(rows[base + t] * BLK, BLK)
            out[t] = coef[:, pl.ds(start, BLK)]
            return 0

        lax.fori_loop(0, slots, step, 0, unroll=4)


def coef_pick(me, coef_t, rows, after, groups):
    slots, occ = rows.shape[0] // groups, coef_t.shape[0]
    return pl.pallas_call(
        coef_pick_kernel,
        out_shape=[jax.ShapeDtypeStruct((slots, occ, BLK), BF)] * groups,
        in_specs=[SMEM, SMEM, VMEM, ANY],
        out_specs=[VMEM] * groups,
        compiler_params=params(16),
        cost_estimate=cost(4 << 20),
        name="coef_pick",
    )(me, rows, coef_t, after)


def coef_join_kernel(me, pos, *rest):
    pieces, out, held = rest[:-2], rest[-2], rest[-1]
    groups, owned = len(pieces), out.shape[0]
    for k, piece in enumerate(pieces):
        held[turn(me[0], -k, groups)] = piece[...]

    def step(k, _):
        parts = []
        for s in range(groups):
            p = pos[s * owned + k]
            block = held[s, jnp.maximum(p, 0)]
            parts.append(jnp.where(p >= 0, block, jnp.zeros_like(block)))
        out[k] = jnp.concatenate(parts, axis=0).T
        return 0

    lax.fori_loop(0, owned, step, 0, unroll=2)


def coef_join(me, pieces, pos, owned):
    groups = len(pieces)
    slots, occ, _ = pieces[0].shape
    return pl.pallas_call(
        coef_join_kernel,
        out_shape=jax.ShapeDtypeStruct((owned, BLK, groups * occ), BF),
        in_specs=[SMEM, SMEM] + [VMEM] * groups,
        out_specs=VMEM,
        scratch_shapes=[pltpu.VMEM((groups, slots, occ, BLK), BF)],
        compiler_params=params(16),
        cost_estimate=cost(4 << 20),
        name="coef_join",
    )(me, pos, *pieces)


def plane_split_kernel(batch, at, pairs, *rest):
    outs, sems = rest[:-1], rest[-1]
    copies = []
    for k, out in enumerate(outs):
        px = turn(at[0], k // NCORE, NX)
        pc = at[1] if k % NCORE == 0 else 1 - at[1]
        copies.append(pltpu.make_async_copy(pairs.at[batch, :, px, pc], out, sems.at[k]))
    for copy in copies:
        copy.start()
    for copy in copies:
        copy.wait()


def plane_split(batch, at, pairs):
    _, nz, nx, nc, occ, width = pairs.shape
    return pl.pallas_call(
        functools.partial(plane_split_kernel, batch),
        out_shape=[jax.ShapeDtypeStruct((nz, occ, width), BF)] * (nx * nc),
        in_specs=[SMEM, pl.BlockSpec(memory_space=pltpu.HBM)],
        out_specs=[VMEM] * (nx * nc),
        scratch_shapes=[pltpu.SemaphoreType.DMA((nx * nc,))],
        compiler_params=params(8),
        cost_estimate=cost(4 << 20),
        name=f"plane_split{batch}",
    )(at, pairs)


def plane_pack_kernel(batch, pairs, *rest):
    out, sems = rest[-2:]
    copies = [
        pltpu.make_async_copy(pairs.at[batch, :, k // NCORE, k % NCORE], out.at[k], sems.at[k])
        for k in range(NX * NCORE)
    ]
    for copy in copies:
        copy.start()
    for copy in copies:
        copy.wait()


def plane_pack(batch, pairs, after):
    _, nz, nx, nc, occ, width = pairs.shape
    return pl.pallas_call(
        functools.partial(plane_pack_kernel, batch),
        out_shape=jax.ShapeDtypeStruct((nx * nc, nz, occ, width), BF),
        in_specs=[pl.BlockSpec(memory_space=pltpu.HBM)] + [ANY] * len(after),
        out_specs=VMEM,
        scratch_shapes=[pltpu.SemaphoreType.DMA((nx * nc,))],
        compiler_params=params(8),
        cost_estimate=cost(4 << 20),
        name="plane_pack",
    )(pairs, *after)


def listed_tiles(out_of, count, listed, got, tiles):
    width = got.shape[3]
    blocks = tiles.shape[1]

    def cut(pz, _):
        for j in range(blocks):
            src, off = divmod(j * BLK, width)
            if off + BLK <= width:
                tiles[pz, j] = got[src, pz, :, off : off + BLK]
            else:
                tiles[pz, j] = jnp.concatenate(
                    [got[src, pz, :, off:width], got[src + 1, pz, :, : off + BLK - width]], axis=1
                )
        return 0

    lax.fori_loop(0, NZ, cut, 0)

    def keep(j, _):
        block = listed[j]
        for k in range(NZ):
            out_of(k, j, block)
        return 0

    lax.fori_loop(0, count, keep, 0)


def all_pack_kernel(pairs, out, sems):
    copies = [
        pltpu.make_async_copy(pairs.at[b], out.at[:, :, :, b], sems.at[b])
        for b in range(pairs.shape[0])
    ]
    for copy in copies:
        copy.start()
    for copy in copies:
        copy.wait()


def all_pack(pairs):
    nb, nz, nx, nc, occ, width = pairs.shape
    hbm = pl.BlockSpec(memory_space=pltpu.HBM)
    return pl.pallas_call(
        all_pack_kernel,
        out_shape=jax.ShapeDtypeStruct((nz, nx, nc, nb, occ, width), BF),
        in_specs=[hbm],
        out_specs=hbm,
        scratch_shapes=[pltpu.SemaphoreType.DMA((nb,))],
        compiler_params=params(8),
        name="all_pack",
    )(pairs)


def plane_pick_turned_kernel(at, listed, *rest):
    n = NX * NCORE
    pieces, outs, (got, tiles) = rest[:n], rest[n + 1 : -3], rest[-2:]
    for k, piece in enumerate(pieces):
        sx = turn(at[0], -(k // NCORE), NX)
        sc = at[1] if k % NCORE == 0 else 1 - at[1]
        got[sx * NCORE + sc] = piece[...]

    def put(k, j, block):
        outs[k][j] = tiles[turn(at[2], k, NZ), block]

    listed_tiles(put, outs[0].shape[0], listed, got, tiles)


def plane_pick_turned(at, listed, pieces, later, cap):
    nz, occ, width = pieces[0].shape
    n = len(pieces)
    return pl.pallas_call(
        plane_pick_turned_kernel,
        out_shape=[jax.ShapeDtypeStruct((cap, occ, BLK), BF)] * nz
        + [jax.ShapeDtypeStruct(later.shape, later.dtype)],
        in_specs=[SMEM, SMEM] + [VMEM] * n + [ANY],
        out_specs=[VMEM] * nz + [ANY],
        input_output_aliases={2 + n: nz},
        scratch_shapes=[
            pltpu.VMEM((n, nz, occ, width), BF),
            pltpu.VMEM((nz, n * width // BLK, occ, BLK), BF),
        ],
        compiler_params=params(24),
        cost_estimate=cost(4 << 20),
        name="plane_pick_turned",
    )(at, listed, *pieces, later)


def plane_pick_kernel(listed, got, *rest):
    out, tiles = rest[-2:]

    def put(k, j, block):
        out[k, j] = tiles[k, block]

    listed_tiles(put, out.shape[1], listed, got, tiles)


def plane_pick(listed, got, cap, after):
    n, nz, occ, width = got.shape
    return pl.pallas_call(
        plane_pick_kernel,
        out_shape=jax.ShapeDtypeStruct((nz, cap, occ, BLK), BF),
        in_specs=[SMEM, VMEM] + [ANY] * len(after),
        out_specs=VMEM,
        scratch_shapes=[pltpu.VMEM((nz, n * width // BLK, occ, BLK), BF)],
        compiler_params=params(20),
        cost_estimate=cost(4 << 20),
        name="plane_pick",
    )(listed, got, *after)


def slot_pick_kernel(me, plane, rank, after, *rest):
    if len(rest) <= NZ:
        got, outs = rest[0], rest[1:]
    else:
        pieces, outs, got = rest[:NZ], rest[NZ:-1], rest[-1]
        for k, piece in enumerate(pieces):
            got[turn(me[1], -k, NZ)] = piece[...]
    slots = outs[0].shape[0]
    for k, out in enumerate(outs):
        base = turn(me[0], k, len(outs)) * slots

        def step(t, _):
            out[t] = got[plane[base + t], rank[base + t]]
            return 0

        lax.fori_loop(0, slots, step, 0, unroll=4)


def slot_pick(me, plane, rank, got, after, groups):
    pieces = got if isinstance(got, list) else [got]
    slots = plane.shape[0] // groups
    cap, occ, _ = pieces[0].shape[-3:]
    turned = len(pieces) > 1
    return pl.pallas_call(
        slot_pick_kernel,
        out_shape=[jax.ShapeDtypeStruct((slots, occ, BLK), BF)] * groups,
        in_specs=[SMEM, SMEM, SMEM, ANY] + [VMEM] * len(pieces),
        out_specs=[VMEM] * groups,
        scratch_shapes=[pltpu.VMEM((NZ, cap, occ, BLK), BF)] if turned else [],
        compiler_params=params(16),
        cost_estimate=cost(2 << 20),
        name="slot_pick",
    )(me, plane, rank, after, *pieces)


def product_kernel(per, groups, me, pos, coef, *rest):
    gamma, (out, held) = rest[:groups], rest[-2:]
    owned = pos.shape[0] // groups
    step = pl.program_id(0)

    @pl.when(step == 0)
    def _():
        for k in range(groups):
            held[turn(me[0], -k, groups)] = gamma[k][...]

    for j in range(per):
        at = [jnp.maximum(pos[s * owned + step * per + j], 0) for s in range(groups)]
        cols = jnp.concatenate([held[s, at[s]] for s in range(groups)], axis=0)
        total = jnp.dot(coef[j], cols, preferred_element_type=jnp.float32)
        out[0, 0, j] = total.astype(BF)


def product(batch, batches, me, coef, gamma, pos, prior):
    owned = coef.shape[0]
    groups = len(gamma)
    per = 20
    extra = [] if prior is None else [prior]
    return pl.pallas_call(
        functools.partial(product_kernel, per, groups),
        out_shape=jax.ShapeDtypeStruct((batches, 1, owned, BLK, BLK), BF),
        grid_spec=pltpu.PrefetchScalarGridSpec(
            num_scalar_prefetch=2,
            grid=(owned // per,),
            in_specs=[pl.BlockSpec((per, BLK, coef.shape[2]), lambda i, *_: (i, 0, 0))]
            + [pl.BlockSpec(gamma[0].shape, lambda i, *_: (0, 0, 0))] * groups
            + [ANY] * len(extra),
            out_specs=pl.BlockSpec((1, 1, per, BLK, BLK), lambda i, *_: (batch, 0, i, 0, 0)),
            scratch_shapes=[pltpu.VMEM((groups,) + gamma[0].shape, BF)],
        ),
        input_output_aliases={3 + groups: 0} if extra else {},
        compiler_params=params(16),
        cost_estimate=cost(6 << 20, 2 * owned * BLK**3),
        name=f"product{batch}",
    )(me, pos, coef, *gamma, *extra)


def local(gamma_pairs, occ_coef, block_lists, block_counts, block_coords):
    batches, aux, occ, width = gamma_pairs.shape
    groups = lax.axis_size("sp")
    basis = occ_coef.shape[0]
    nblk = basis // BLK
    per_plane = nblk // NZ
    plane_devs = NX * NCORE
    total_blocks = block_coords.shape[0]
    owned = total_blocks // groups
    capacity = block_lists.shape[2]
    me_s = lax.axis_index("sp")
    me_z = lax.axis_index("z")

    at = jnp.stack([lax.axis_index(name) for name in ("x", "core", "z")]).astype(jnp.int32)
    pairs = gamma_pairs.reshape(batches, NZ, NX, NCORE, occ, width)
    pairs = pltpu.with_memory_space_constraint(pairs, pltpu.HBM)

    def exchange_plane(split):
        got = [split[0]]
        for k in range(1, plane_devs):
            dx, dc = divmod(k, NCORE)
            moves = [
                (x * NCORE + c, (x + dx) % NX * NCORE + (c ^ dc))
                for x in range(NX)
                for c in range(NCORE)
            ]
            got.append(lax.ppermute(split[k], ("x", "core"), moves))
        return got

    got0 = exchange_plane(plane_split(0, at, pairs))
    packed1 = plane_pack(1, pairs, got0[1:2])

    valid = jnp.arange(capacity, dtype=jnp.int32)[None, None, :] < block_counts[:, :, None]
    lists = jnp.clip(block_lists, 0, owned - 1)
    ids = lists + (jnp.arange(groups, dtype=jnp.int32) * owned)[None, :, None]
    hit = ids.reshape(groups, -1, 1) == jnp.arange(total_blocks, dtype=jnp.int32)
    row_ids = jnp.sum(jnp.where(hit, block_coords[:, 0], 0), axis=2)
    col_ids = jnp.sum(jnp.where(hit, block_coords[:, 1], 0), axis=2)
    live_col = jnp.where(valid.reshape(groups, -1), col_ids, -1)
    need = jnp.any(live_col[:, :, None] == jnp.arange(nblk, dtype=jnp.int32), axis=1)
    need = need.reshape(groups, NZ, per_plane).astype(jnp.int32)
    most = jnp.max(jnp.sum(need, axis=2))
    my_need = lax.dynamic_index_in_dim(need, me_s, 0, keepdims=False)
    plane_ids = jnp.arange(per_plane, dtype=jnp.int32)
    before = (plane_ids[None, :] < plane_ids[:, None]).astype(jnp.int32)
    rank = jnp.sum(my_need[:, None, :] * before[None], axis=2)
    my_cols = lax.dynamic_index_in_dim(col_ids, me_s, 0, keepdims=False)
    my_rows = lax.dynamic_index_in_dim(row_ids, me_s, 0, keepdims=False)
    my_live = lax.dynamic_index_in_dim(valid.reshape(groups, -1), me_s, 0, keepdims=False)
    col_hit = my_cols[:, None] == jnp.arange(nblk, dtype=jnp.int32)
    slot_rank = jnp.sum(jnp.where(col_hit, rank.reshape(-1), 0), axis=1)
    slot_rank = jnp.where(my_live, slot_rank, 0)
    slot_plane = jnp.where(my_live, my_cols // per_plane, 0)
    plane_need = lax.dynamic_index_in_dim(my_need, me_z, 0, keepdims=False)
    plane_rank = lax.dynamic_index_in_dim(rank, me_z, 0, keepdims=False)
    listed = jnp.sum(
        jnp.where(
            (plane_rank[None, :] == plane_ids[:, None]) & (plane_need[None, :] > 0),
            plane_ids[None, :],
            0,
        ),
        axis=1,
    )
    to_me = lax.dynamic_index_in_dim(lists, me_s, 1, keepdims=False)
    to_me_valid = lax.dynamic_index_in_dim(valid, me_s, 1, keepdims=False)
    hits = (to_me[:, None, :] == jnp.arange(owned, dtype=jnp.int32)[None, :, None]) & to_me_valid[
        :, None, :
    ]
    slot_no = jnp.arange(capacity, dtype=jnp.int32) + 1
    pos = (jnp.sum(jnp.where(hits, slot_no, 0), axis=2) - 1).reshape(-1)

    me = jnp.stack([me_s, me_z]).astype(jnp.int32)
    def exchange_owners(sent):
        return [sent[0]] + [
            lax.ppermute(sent[k], "sp", [(i, (i + k) % groups) for i in range(groups)])
            for k in range(1, groups)
        ]

    listed = listed[:CAP]
    slot_at = jnp.minimum(slot_rank, CAP - 1)

    *sent0, packed1 = plane_pick_turned(at, listed, got0, packed1, CAP)
    got1 = lax.all_to_all(packed1, ("x", "core"), 0, 0, tiled=True)
    held0 = [sent0[0]] + [
        lax.ppermute(sent0[k], "z", [(i, (i + k) % NZ) for i in range(NZ)]) for k in range(1, NZ)
    ]
    parts0 = slot_pick(me, slot_plane, slot_at, held0, me, groups)
    coef_parts = exchange_owners(coef_pick(me, occ_coef.T, my_rows, parts0[0], groups))
    coef = coef_join(me, coef_parts, pos, owned)
    held1 = lax.all_to_all(plane_pick(listed, got1, CAP, held0[1:]), "z", 0, 0, tiled=True)
    out = product(0, batches, me, coef, exchange_owners(parts0), pos, None)
    parts1 = slot_pick(me, slot_plane, slot_at, held1, out[0, 0, 0, :8], groups)
    out = product(1, batches, me, coef, exchange_owners(parts1), pos, out)

    def all_columns(out):
        packed = all_pack(pairs).reshape(NZ * plane_devs, batches, occ, width)
        gathered = lax.all_to_all(packed, ("z", "x", "core"), 0, 0, tiled=True)
        blocks = gathered.transpose(1, 2, 0, 3).reshape(batches, occ, nblk, BLK)
        taken = jnp.take(blocks, my_cols, axis=2).transpose(0, 2, 1, 3)
        for b in range(batches):
            sent = taken[b].reshape(groups, capacity, occ, BLK)
            gamma = lax.all_to_all(sent, "sp", 0, 0, tiled=True)
            parts = [
                lax.dynamic_index_in_dim(gamma, (me_s - k + groups) % groups, 0, keepdims=False)
                for k in range(groups)
            ]
            out = product(b, batches, me, coef, parts, pos, out)
        return out

    return lax.cond(most > CAP, all_columns, lambda out: out, out)


def solution(mesh):
    groups = mesh.shape["sp"]
    grid = Mesh(mesh.devices.reshape(NZ, NX, NCORE, groups), ("z", "x", "core", "sp"))
    pair = ("z", "x", "core")
    in_specs = (P(None, None, "sp", pair), P(None, "sp"), P(), P(), P())
    out_specs = P(None, pair, "sp", None, None)
    return jax.shard_map(local, mesh=grid, in_specs=in_specs, out_specs=out_specs, check_vma=False)
```

```python
import functools

import jax
import jax.numpy as jnp
from jax import lax
from jax.experimental import pallas as pl
from jax.experimental.pallas import tpu as pltpu
from jax.sharding import Mesh, PartitionSpec as P

BLK = 128
NZ, NX, NCORE = 8, 4, 2
LEVELS = (5, 6, 8)
BF = jnp.bfloat16
VMEM = pl.BlockSpec(memory_space=pltpu.VMEM)
ANY = pl.BlockSpec(memory_space=pl.ANY)
SMEM = pl.BlockSpec(memory_space=pltpu.SMEM)


def params(mib):
    return pltpu.CompilerParams(vmem_limit_bytes=mib << 20)


def cost(nbytes, flops=0):
    return pl.CostEstimate(flops=flops, bytes_accessed=nbytes, transcendentals=0)


def turn(start, k, n):
    at = start + k
    at = jnp.where(at >= n, at - n, at)
    return jnp.where(at < 0, at + n, at)


def coef_pick_kernel(me, rows, coef, after, *outs):
    slots = outs[0].shape[0]
    for k, out in enumerate(outs):
        base = turn(me[0], k, len(outs)) * slots

        def step(t, _):
            start = pl.multiple_of(rows[base + t] * BLK, BLK)
            out[t] = coef[:, pl.ds(start, BLK)]
            return 0

        lax.fori_loop(0, slots, step, 0, unroll=4)


def coef_pick(me, coef_t, rows, after, groups):
    slots, occ = rows.shape[0] // groups, coef_t.shape[0]
    return pl.pallas_call(
        coef_pick_kernel,
        out_shape=[jax.ShapeDtypeStruct((slots, occ, BLK), BF)] * groups,
        in_specs=[SMEM, SMEM, VMEM, ANY],
        out_specs=[VMEM] * groups,
        compiler_params=params(16),
        cost_estimate=cost(4 << 20),
        name="coef_pick",
    )(me, rows, coef_t, after)


def coef_join_kernel(me, pos, *rest):
    pieces, out, held = rest[:-2], rest[-2], rest[-1]
    groups, owned = len(pieces), out.shape[0]
    for k, piece in enumerate(pieces):
        held[turn(me[0], -k, groups)] = piece[...]

    def step(k, _):
        parts = []
        for s in range(groups):
            p = pos[s * owned + k]
            block = held[s, jnp.maximum(p, 0)]
            parts.append(jnp.where(p >= 0, block, jnp.zeros_like(block)))
        out[k] = jnp.concatenate(parts, axis=0).T
        return 0

    lax.fori_loop(0, owned, step, 0, unroll=2)


def coef_join(me, pieces, pos, owned):
    groups = len(pieces)
    slots, occ, _ = pieces[0].shape
    return pl.pallas_call(
        coef_join_kernel,
        out_shape=jax.ShapeDtypeStruct((owned, BLK, groups * occ), BF),
        in_specs=[SMEM, SMEM] + [VMEM] * groups,
        out_specs=VMEM,
        scratch_shapes=[pltpu.VMEM((groups, slots, occ, BLK), BF)],
        compiler_params=params(16),
        cost_estimate=cost(4 << 20),
        name="coef_join",
    )(me, pos, *pieces)


def core_split_kernel(at, pairs, *rest):
    outs, sems = rest[:-1], rest[-1]
    copies = []
    for k, out in enumerate(outs):
        core = at[1] if k % 2 == 0 else 1 - at[1]
        copies.append(pltpu.make_async_copy(pairs.at[k // 2, :, :, core], out, sems.at[k]))
    for copy in copies:
        copy.start()
    for copy in copies:
        copy.wait()


def core_split(at, pairs):
    nb, nz, nx, _, occ, width = pairs.shape
    return pl.pallas_call(
        core_split_kernel,
        out_shape=[jax.ShapeDtypeStruct((nz, nx, occ, width), BF)] * (2 * nb),
        in_specs=[SMEM, pl.BlockSpec(memory_space=pltpu.HBM)],
        out_specs=[VMEM] * (2 * nb),
        scratch_shapes=[pltpu.SemaphoreType.DMA((2 * nb,))],
        compiler_params=params(12),
        cost_estimate=cost(8 << 20),
        name="core_split",
    )(at, pairs)


def cut_tiles(odd, left, right, tiles):
    nz, nx, occ, width = left.shape

    def row(i, _):
        z, x = i // nx, i % nx

        def span(lo, hi):
            parts = []
            if lo < width:
                parts.append(left[z, x, :, lo : min(hi, width)])
            if hi > width:
                parts.append(right[z, x, :, max(lo, width) - width : hi - width])
            return parts

        half = [jnp.zeros((occ, BLK // 2), BF)]
        for t in range(tiles.shape[1]):
            lo = t * BLK - (BLK // 2 if odd else 0)
            hi = lo + BLK
            parts = span(max(lo, 0), min(hi, 2 * width))
            if lo < 0:
                parts = half + parts
            if hi > 2 * width:
                parts = parts + half
            tiles[i, t] = parts[0] if len(parts) == 1 else jnp.concatenate(parts, axis=1)
        return 0

    lax.fori_loop(0, nz * nx, row, 0)


def tile_pick_kernel(at, listed, own, got, after, out, tiles):
    for odd in (0, 1):
        for core in (0, 1):
            left, right = (own, got) if core == 0 else (got, own)

            @pl.when((at[0] % 2 == odd) & (at[1] == core))
            def _():
                cut_tiles(odd, left, right, tiles)

    def keep(i, _):
        for j in range(out.shape[1]):
            out[i, j] = tiles[i, listed[j]]
        return 0

    lax.fori_loop(0, out.shape[0], keep, 0, unroll=2)


def tile_pick(at, listed, own, got, after, cap):
    nz, nx, occ, width = own.shape
    held = -(-2 * width // BLK)
    return pl.pallas_call(
        tile_pick_kernel,
        out_shape=jax.ShapeDtypeStruct((nz * nx, cap, occ, BLK), BF),
        in_specs=[SMEM, SMEM, VMEM, VMEM, ANY],
        out_specs=VMEM,
        scratch_shapes=[pltpu.VMEM((nz * nx, held, occ, BLK), BF)],
        compiler_params=params(16),
        cost_estimate=cost(4 << 20),
        name="tile_pick",
    )(at, listed, own, got, after)


def slot_pick_kernel(me, first, second, got, *outs):
    cap = got.shape[1]
    slots, occ, _ = outs[0].shape
    low = lax.broadcasted_iota(jnp.int32, (occ, BLK), 1) < BLK // 2
    for k, out in enumerate(outs):
        base = turn(me[0], k, len(outs)) * slots

        def step(t, _):
            a, b = first[base + t], second[base + t]
            out[t] = jnp.where(low, got[a // cap, a % cap], got[b // cap, b % cap])
            return 0

        lax.fori_loop(0, slots, step, 0, unroll=4)


def slot_pick(me, first, second, got, groups):
    slots = first.shape[0] // groups
    occ = got.shape[2]
    return pl.pallas_call(
        slot_pick_kernel,
        out_shape=[jax.ShapeDtypeStruct((slots, occ, BLK), BF)] * groups,
        in_specs=[SMEM, SMEM, SMEM, VMEM],
        out_specs=[VMEM] * groups,
        compiler_params=params(16),
        cost_estimate=cost(2 << 20),
        name="slot_pick",
    )(me, first, second, got)


def product_kernel(per, groups, me, pos, coef, *rest):
    gamma, (out, held) = rest[:groups], rest[-2:]
    owned = pos.shape[0] // groups
    step = pl.program_id(0)

    @pl.when(step == 0)
    def _():
        for k in range(groups):
            held[turn(me[0], -k, groups)] = gamma[k][...]

    for j in range(per):
        at = [jnp.maximum(pos[s * owned + step * per + j], 0) for s in range(groups)]
        cols = jnp.concatenate([held[s, at[s]] for s in range(groups)], axis=0)
        total = jnp.dot(coef[j], cols, preferred_element_type=jnp.float32)
        out[0, 0, j] = total.astype(BF)


def product(batch, batches, me, coef, gamma, pos, prior):
    owned = coef.shape[0]
    groups = len(gamma)
    per = 20
    extra = [] if prior is None else [prior]
    return pl.pallas_call(
        functools.partial(product_kernel, per, groups),
        out_shape=jax.ShapeDtypeStruct((batches, 1, owned, BLK, BLK), BF),
        grid_spec=pltpu.PrefetchScalarGridSpec(
            num_scalar_prefetch=2,
            grid=(owned // per,),
            in_specs=[pl.BlockSpec((per, BLK, coef.shape[2]), lambda i, *_: (i, 0, 0))]
            + [pl.BlockSpec(gamma[0].shape, lambda i, *_: (0, 0, 0))] * groups
            + [ANY] * len(extra),
            out_specs=pl.BlockSpec((1, 1, per, BLK, BLK), lambda i, *_: (batch, 0, i, 0, 0)),
            scratch_shapes=[pltpu.VMEM((groups,) + gamma[0].shape, BF)],
        ),
        input_output_aliases={3 + groups: 0} if extra else {},
        compiler_params=params(16),
        cost_estimate=cost(6 << 20, 2 * owned * BLK**3),
        name=f"product{batch}",
    )(me, pos, coef, *gamma, *extra)


def local(gamma_pairs, occ_coef, block_lists, block_counts, block_coords):
    batches, aux, occ, width = gamma_pairs.shape
    groups = lax.axis_size("sp")
    basis = occ_coef.shape[0]
    nblk = basis // BLK
    total_blocks = block_coords.shape[0]
    owned = total_blocks // groups
    capacity = block_lists.shape[2]
    me_s = lax.axis_index("sp")
    me_z = lax.axis_index("z")

    at = jnp.stack([lax.axis_index("x"), lax.axis_index("core")]).astype(jnp.int32)
    pairs = gamma_pairs.reshape(batches, NZ, NX, NCORE, occ, width)

    pairs = pltpu.with_memory_space_constraint(pairs, pltpu.HBM)

    halves = core_split(at, pairs)
    halves0, halves1 = (
        (halves[2 * b], lax.ppermute(halves[2 * b + 1], "core", [(0, 1), (1, 0)]))
        for b in range(batches)
    )

    valid = jnp.arange(capacity, dtype=jnp.int32)[None, None, :] < block_counts[:, :, None]
    lists = jnp.clip(block_lists, 0, owned - 1)
    ids = lists + (jnp.arange(groups, dtype=jnp.int32) * owned)[None, :, None]
    hit = ids.reshape(groups, -1, 1) == jnp.arange(total_blocks, dtype=jnp.int32)
    row_ids = jnp.sum(jnp.where(hit, block_coords[:, 0], 0), axis=2)
    col_ids = jnp.sum(jnp.where(hit, block_coords[:, 1], 0), axis=2)
    live_col = jnp.where(valid.reshape(groups, -1), col_ids, -1)
    need = jnp.any(live_col[:, :, None] == jnp.arange(nblk, dtype=jnp.int32), axis=1)
    pair_blocks = 2 * nblk // (NZ * NX)
    held = -(-2 * width // BLK)
    need = need.reshape(groups, NZ * NX // 2, 1, pair_blocks).astype(jnp.int32)
    need = jnp.concatenate([need[..., :held], need[..., pair_blocks - held :]], axis=2)
    need = need.reshape(groups, NZ * NX, held)
    most = jnp.max(jnp.sum(need, axis=2))
    my_need = lax.dynamic_index_in_dim(need, me_s, 0, keepdims=False)
    tile_ids = jnp.arange(held, dtype=jnp.int32)
    before = (tile_ids[None, :] < tile_ids[:, None]).astype(jnp.int32)
    rank = jnp.sum(my_need[:, None, :] * before[None], axis=2)
    my_cols = lax.dynamic_index_in_dim(col_ids, me_s, 0, keepdims=False)
    my_rows = lax.dynamic_index_in_dim(row_ids, me_s, 0, keepdims=False)
    my_live = lax.dynamic_index_in_dim(valid.reshape(groups, -1), me_s, 0, keepdims=False)
    two_chips, within = my_cols // pair_blocks, my_cols % pair_blocks

    def place(upper):
        on_odd = within > held - 1 - upper
        chip = 2 * two_chips + on_odd
        tile = within - jnp.where(on_odd, pair_blocks - held, 0)
        hit = (chip * held + tile)[:, None] == jnp.arange(NZ * NX * held, dtype=jnp.int32)
        order = jnp.sum(jnp.where(hit, rank.reshape(-1), 0), axis=1)
        return jnp.where(my_live, chip, 0), jnp.where(my_live, order, 0)

    chip_a, rank_a = place(0)
    chip_b, rank_b = place(1)
    my_chip = me_z * NX + lax.axis_index("x")
    chip_need = lax.dynamic_index_in_dim(my_need, my_chip, 0, keepdims=False)
    chip_rank = lax.dynamic_index_in_dim(rank, my_chip, 0, keepdims=False)
    listed = jnp.sum(
        jnp.where(
            (chip_rank[None, :] == tile_ids[:, None]) & (chip_need[None, :] > 0),
            tile_ids[None, :],
            0,
        ),
        axis=1,
    )
    to_me = lax.dynamic_index_in_dim(lists, me_s, 1, keepdims=False)
    to_me_valid = lax.dynamic_index_in_dim(valid, me_s, 1, keepdims=False)
    hits = (to_me[:, None, :] == jnp.arange(owned, dtype=jnp.int32)[None, :, None]) & to_me_valid[
        :, None, :
    ]
    slot_no = jnp.arange(capacity, dtype=jnp.int32) + 1
    pos = (jnp.sum(jnp.where(hits, slot_no, 0), axis=2) - 1).reshape(-1)

    me = me_s[None].astype(jnp.int32)
    def exchange_owners(sent):
        return [sent[0]] + [
            lax.ppermute(sent[k], "sp", [(i, (i + k) % groups) for i in range(groups)])
            for k in range(1, groups)
        ]

    def finish(cap, halves0, halves1, coef_t, my_rows, pos, listed, chip_a, rank_a, chip_b, rank_b):
        first, second = chip_a * cap + rank_a, chip_b * cap + rank_b

        def tiles(halves, after):
            picked = tile_pick(at, listed, *halves, after, cap)
            return picked, lax.all_to_all(picked, ("z", "x"), 0, 0, tiled=True)

        def owners(got):
            return exchange_owners(slot_pick(me, first, second, got, groups))

        picked0, got0 = tiles(halves0, me)
        coef_parts = exchange_owners(coef_pick(me, coef_t, my_rows, picked0, groups))
        coef = coef_join(me, coef_parts, pos, owned)
        _, got1 = tiles(halves1, coef)
        out = product(0, batches, me, coef, owners(got0), pos, None)
        return product(1, batches, me, coef, owners(got1), pos, out)

    level = jnp.sum((most > jnp.array(LEVELS[:-1], jnp.int32)).astype(jnp.int32))
    level, listed = lax.optimization_barrier((level, listed))
    tables = (my_rows, pos, listed, chip_a, rank_a, chip_b, rank_b)
    branches = [functools.partial(finish, cap) for cap in LEVELS]
    return lax.switch(level, branches, halves0, halves1, occ_coef.T, *tables)


def solution(mesh):
    groups = mesh.shape["sp"]
    grid = Mesh(mesh.devices.reshape(NZ, NX, NCORE, groups), ("z", "x", "core", "sp"))
    pair = ("z", "x", "core")
    in_specs = (P(None, None, "sp", pair), P(None, "sp"), P(), P(), P())
    out_specs = P(None, pair, "sp", None, None)
    return jax.shard_map(local, mesh=grid, in_specs=in_specs, out_specs=out_specs, check_vma=False)
```

```python
import functools

import jax
import jax.numpy as jnp
from jax import lax
from jax.experimental import pallas as pl
from jax.experimental.pallas import tpu as pltpu
from jax.sharding import Mesh, PartitionSpec as P

BLK = 128
NZ, NX, NCORE = 8, 4, 2
LEVELS = (5, 6, 8)
BF = jnp.bfloat16
VMEM = pl.BlockSpec(memory_space=pltpu.VMEM)
ANY = pl.BlockSpec(memory_space=pl.ANY)
SMEM = pl.BlockSpec(memory_space=pltpu.SMEM)


def params(mib):
    return pltpu.CompilerParams(vmem_limit_bytes=mib << 20)


def cost(nbytes, flops=0):
    return pl.CostEstimate(flops=flops, bytes_accessed=nbytes, transcendentals=0)


def turn(start, k, n):
    at = start + k
    at = jnp.where(at >= n, at - n, at)
    return jnp.where(at < 0, at + n, at)


def coef_pick_kernel(me, rows, coef, after, *outs):
    slots = outs[0].shape[0]
    for k, out in enumerate(outs):
        base = turn(me[0], k, len(outs)) * slots

        def step(t, _):
            start = pl.multiple_of(rows[base + t] * BLK, BLK)
            out[t] = coef[:, pl.ds(start, BLK)]
            return 0

        lax.fori_loop(0, slots, step, 0, unroll=4)


def coef_pick(me, coef_t, rows, after, groups):
    slots, occ = rows.shape[0] // groups, coef_t.shape[0]
    return pl.pallas_call(
        coef_pick_kernel,
        out_shape=[jax.ShapeDtypeStruct((slots, occ, BLK), BF)] * groups,
        in_specs=[SMEM, SMEM, VMEM, ANY],
        out_specs=[VMEM] * groups,
        compiler_params=params(16),
        cost_estimate=cost(4 << 20),
        name="coef_pick",
    )(me, rows, coef_t, after)


def coef_join_kernel(me, pos, *rest):
    pieces, out, held = rest[:-2], rest[-2], rest[-1]
    groups, owned = len(pieces), out.shape[0]
    for k, piece in enumerate(pieces):
        held[turn(me[0], -k, groups)] = piece[...]

    def step(k, _):
        parts = []
        for s in range(groups):
            p = pos[s * owned + k]
            block = held[s, jnp.maximum(p, 0)]
            parts.append(jnp.where(p >= 0, block, jnp.zeros_like(block)))
        out[k] = jnp.concatenate(parts, axis=0).T
        return 0

    lax.fori_loop(0, owned, step, 0, unroll=2)


def coef_join(me, pieces, pos, owned):
    groups = len(pieces)
    slots, occ, _ = pieces[0].shape
    return pl.pallas_call(
        coef_join_kernel,
        out_shape=jax.ShapeDtypeStruct((owned, BLK, groups * occ), BF),
        in_specs=[SMEM, SMEM] + [VMEM] * groups,
        out_specs=VMEM,
        scratch_shapes=[pltpu.VMEM((groups, slots, occ, BLK), BF)],
        compiler_params=params(16),
        cost_estimate=cost(4 << 20),
        name="coef_join",
    )(me, pos, *pieces)


def core_split_kernel(at, pairs, *rest):
    outs, sems = rest[:-1], rest[-1]
    copies = []
    for k, out in enumerate(outs):
        core = at[1] if k % 2 == 0 else 1 - at[1]
        copies.append(pltpu.make_async_copy(pairs.at[k // 2, :, :, core], out, sems.at[k]))
    for copy in copies:
        copy.start()
    for copy in copies:
        copy.wait()


def core_split(at, pairs):
    nb, nz, nx, _, occ, width = pairs.shape
    return pl.pallas_call(
        core_split_kernel,
        out_shape=[jax.ShapeDtypeStruct((nz, nx, occ, width), BF)] * (2 * nb),
        in_specs=[SMEM, pl.BlockSpec(memory_space=pltpu.HBM)],
        out_specs=[VMEM] * (2 * nb),
        scratch_shapes=[pltpu.SemaphoreType.DMA((2 * nb,))],
        compiler_params=params(12),
        cost_estimate=cost(8 << 20),
        name="core_split",
    )(at, pairs)


def cut_tile(odd, t, left, right, out, j):
    rows, occ, width = left.shape
    lo = t * BLK - (BLK // 2 if odd else 0)
    first, last = max(lo, 0), min(lo + BLK, 2 * width)

    def row(i, _):
        parts = []
        if lo < 0:
            parts.append(jnp.zeros((occ, -lo), BF))
        if first < width:
            parts.append(left[i, :, first : min(last, width)])
        if last > width:
            parts.append(right[i, :, max(first, width) - width : last - width])
        if last < lo + BLK:
            parts.append(jnp.zeros((occ, lo + BLK - last), BF))
        out[i, j] = parts[0] if len(parts) == 1 else jnp.concatenate(parts, axis=1)
        return 0

    lax.fori_loop(0, rows, row, 0, unroll=2)


def tile_pick_kernel(at, listed, own, got, after, out):
    held = listed.shape[0] - 1
    for odd in (0, 1):
        for core in (0, 1):
            left, right = (own, got) if core == 0 else (got, own)

            @pl.when((at[0] % 2 == odd) & (at[1] == core))
            def _():
                def keep(j, _):
                    for t in range(held):

                        @pl.when(listed[j] == t)
                        def _():
                            cut_tile(odd, t, left, right, out, j)

                    return 0

                lax.fori_loop(0, jnp.minimum(listed[held], out.shape[1]), keep, 0)


def tile_pick(at, listed, own, got, after, cap):
    rows, occ, width = own.shape
    return pl.pallas_call(
        tile_pick_kernel,
        out_shape=jax.ShapeDtypeStruct((rows, cap, occ, BLK), BF),
        in_specs=[SMEM, SMEM, VMEM, VMEM, ANY],
        out_specs=VMEM,
        compiler_params=params(16),
        cost_estimate=cost(4 << 20),
        name="tile_pick",
    )(at, listed, own, got, after)


def slot_pick_kernel(me, spots, got, *outs):
    slots, occ, _ = outs[0].shape
    low = lax.broadcasted_iota(jnp.int32, (occ, BLK), 1) < BLK // 2
    total = len(outs) * slots
    for k, out in enumerate(outs):
        base = turn(me[0], k, len(outs)) * slots

        def step(t, _):
            a, b = spots[base + t], spots[total + base + t]
            out[t] = jnp.where(low, got[a >> 3, a & 7], got[b >> 3, b & 7])
            return 0

        lax.fori_loop(0, slots, step, 0, unroll=10)


def slot_pick(me, spots, got, groups):
    slots = spots.shape[0] // (2 * groups)
    occ = got.shape[2]
    return pl.pallas_call(
        slot_pick_kernel,
        out_shape=[jax.ShapeDtypeStruct((slots, occ, BLK), BF)] * groups,
        in_specs=[SMEM, SMEM, VMEM],
        out_specs=[VMEM] * groups,
        compiler_params=params(16),
        cost_estimate=cost(2 << 20),
        name="slot_pick",
    )(me, spots, got)


def product_kernel(per, groups, me, pos, coef, *rest):
    gamma, (out, held) = rest[:groups], rest[-2:]
    owned = pos.shape[0] // groups
    step = pl.program_id(0)

    @pl.when(step == 0)
    def _():
        for k in range(groups):
            held[turn(me[0], -k, groups)] = gamma[k][...]

    for j in range(per):
        at = [jnp.maximum(pos[s * owned + step * per + j], 0) for s in range(groups)]
        cols = jnp.concatenate([held[s, at[s]] for s in range(groups)], axis=0)
        total = jnp.dot(coef[j], cols, preferred_element_type=jnp.float32)
        out[0, 0, j] = total.astype(BF)


def product(batch, batches, me, coef, gamma, pos, prior):
    owned = coef.shape[0]
    groups = len(gamma)
    per = 20
    extra = [] if prior is None else [prior]
    return pl.pallas_call(
        functools.partial(product_kernel, per, groups),
        out_shape=jax.ShapeDtypeStruct((batches, 1, owned, BLK, BLK), BF),
        grid_spec=pltpu.PrefetchScalarGridSpec(
            num_scalar_prefetch=2,
            grid=(owned // per,),
            in_specs=[pl.BlockSpec((per, BLK, coef.shape[2]), lambda i, *_: (i, 0, 0))]
            + [pl.BlockSpec(gamma[0].shape, lambda i, *_: (0, 0, 0))] * groups
            + [ANY] * len(extra),
            out_specs=pl.BlockSpec((1, 1, per, BLK, BLK), lambda i, *_: (batch, 0, i, 0, 0)),
            scratch_shapes=[pltpu.VMEM((groups,) + gamma[0].shape, BF)],
        ),
        input_output_aliases={3 + groups: 0} if extra else {},
        compiler_params=params(16),
        cost_estimate=cost(6 << 20, 2 * owned * BLK**3),
        name=f"product{batch}",
    )(me, pos, coef, *gamma, *extra)


def local(gamma_pairs, occ_coef, block_lists, block_counts, block_coords):
    batches, aux, occ, width = gamma_pairs.shape
    groups = lax.axis_size("sp")
    basis = occ_coef.shape[0]
    nblk = basis // BLK
    total_blocks = block_coords.shape[0]
    owned = total_blocks // groups
    capacity = block_lists.shape[2]
    me_s = lax.axis_index("sp")
    me_z = lax.axis_index("z")

    at = jnp.stack([lax.axis_index("x"), lax.axis_index("core")]).astype(jnp.int32)
    pairs = gamma_pairs.reshape(batches, NZ, NX, NCORE, occ, width)

    pairs = pltpu.with_memory_space_constraint(pairs, pltpu.HBM)

    halves, block_lists, block_counts, block_coords = lax.optimization_barrier(
        (core_split(at, pairs), block_lists, block_counts, block_coords)
    )
    halves0, halves1 = (
        (halves[2 * b], lax.ppermute(halves[2 * b + 1], "core", [(0, 1), (1, 0)]))
        for b in range(batches)
    )

    valid = jnp.arange(capacity, dtype=jnp.int32)[None, None, :] < block_counts[:, :, None]
    lists = jnp.clip(block_lists, 0, owned - 1)
    ids = lists + (jnp.arange(groups, dtype=jnp.int32) * owned)[None, :, None]
    hit = ids.reshape(groups, -1, 1) == jnp.arange(total_blocks, dtype=jnp.int32)
    row_ids = jnp.sum(jnp.where(hit, block_coords[:, 0], 0), axis=2)
    col_ids = jnp.sum(jnp.where(hit, block_coords[:, 1], 0), axis=2)
    live_col = jnp.where(valid.reshape(groups, -1), col_ids, -1)
    need = jnp.any(live_col[:, :, None] == jnp.arange(nblk, dtype=jnp.int32), axis=1)
    pair_blocks = 2 * nblk // (NZ * NX)
    held = -(-2 * width // BLK)
    need = need.reshape(groups, NZ * NX // 2, 1, pair_blocks).astype(jnp.int32)
    need = jnp.concatenate([need[..., :held], need[..., pair_blocks - held :]], axis=2)
    need = need.reshape(groups, NZ * NX, held)
    most = jnp.max(jnp.sum(need, axis=2))
    my_need = lax.dynamic_index_in_dim(need, me_s, 0, keepdims=False)
    tile_ids = jnp.arange(held, dtype=jnp.int32)
    before = (tile_ids[None, :] < tile_ids[:, None]).astype(jnp.int32)
    rank = jnp.sum(my_need[:, None, :] * before[None], axis=2)
    my_cols = lax.dynamic_index_in_dim(col_ids, me_s, 0, keepdims=False)
    my_rows = lax.dynamic_index_in_dim(row_ids, me_s, 0, keepdims=False)
    my_live = lax.dynamic_index_in_dim(valid.reshape(groups, -1), me_s, 0, keepdims=False)
    slot_cols = my_cols.reshape(groups, capacity)
    slot_cols = jnp.where(my_live.reshape(groups, capacity), slot_cols, slot_cols[:, :1])
    slot_cols = slot_cols.reshape(-1)
    two_chips, within = slot_cols // pair_blocks, slot_cols % pair_blocks
    upper = jnp.arange(2, dtype=jnp.int32)[:, None]
    on_odd = (within[None, :] > held - 1 - upper).astype(jnp.int32)
    chip = 2 * two_chips[None, :] + on_odd
    tile = within[None, :] - on_odd * (pair_blocks - held)
    tile_hit = (chip * held + tile)[:, :, None] == jnp.arange(NZ * NX * held, dtype=jnp.int32)
    order = jnp.sum(jnp.where(tile_hit, rank.reshape(-1), 0), axis=2)
    spots = (8 * chip + order).reshape(-1)
    my_chip = me_z * NX + lax.axis_index("x")
    chip_need = lax.dynamic_index_in_dim(my_need, my_chip, 0, keepdims=False)
    chip_rank = lax.dynamic_index_in_dim(rank, my_chip, 0, keepdims=False)
    listed = jnp.sum(
        jnp.where(
            (chip_rank[None, :] == tile_ids[:, None]) & (chip_need[None, :] > 0),
            tile_ids[None, :],
            0,
        ),
        axis=1,
    )
    listed = jnp.concatenate([listed, jnp.sum(chip_need, keepdims=True)])
    to_me = lax.dynamic_index_in_dim(lists, me_s, 1, keepdims=False)
    to_me_valid = lax.dynamic_index_in_dim(valid, me_s, 1, keepdims=False)
    hits = (to_me[:, None, :] == jnp.arange(owned, dtype=jnp.int32)[None, :, None]) & to_me_valid[
        :, None, :
    ]
    slot_no = jnp.arange(capacity, dtype=jnp.int32) + 1
    pos = (jnp.sum(jnp.where(hits, slot_no, 0), axis=2) - 1).reshape(-1)

    me = me_s[None].astype(jnp.int32)
    def exchange_owners(sent):
        return [sent[0]] + [
            lax.ppermute(sent[k], "sp", [(i, (i + k) % groups) for i in range(groups)])
            for k in range(1, groups)
        ]

    def finish(cap, halves0, halves1, coef_t, my_rows, pos, listed, spots):
        def tiles(halves, after):
            halves = [half.reshape(NZ * NX, occ, width) for half in halves]
            picked = tile_pick(at, listed, *halves, after, cap)
            return picked, lax.all_to_all(picked, ("z", "x"), 0, 0, tiled=True)

        def owners(got):
            return exchange_owners(slot_pick(me, spots, got, groups))

        picked0, got0 = tiles(halves0, me)
        coef_parts = exchange_owners(coef_pick(me, coef_t, my_rows, picked0, groups))
        coef = coef_join(me, coef_parts, pos, owned)
        _, got1 = tiles(halves1, coef)
        out = product(0, batches, me, coef, owners(got0), pos, None)
        return product(1, batches, me, coef, owners(got1), pos, out)

    level = sum((most > cap).astype(jnp.int32) for cap in LEVELS[:-1])
    level, *tables = lax.optimization_barrier((level, my_rows, pos, listed, spots))
    branches = [functools.partial(finish, cap) for cap in LEVELS]
    return lax.switch(level, branches, halves0, halves1, occ_coef.T, *tables)


def solution(mesh):
    groups = mesh.shape["sp"]
    grid = Mesh(mesh.devices.reshape(NZ, NX, NCORE, groups), ("z", "x", "core", "sp"))
    pair = ("z", "x", "core")
    in_specs = (P(None, None, "sp", pair), P(None, "sp"), P(), P(), P())
    out_specs = P(None, pair, "sp", None, None)
    return jax.shard_map(local, mesh=grid, in_specs=in_specs, out_specs=out_specs, check_vma=False)
```

```python
import functools

import jax
import jax.numpy as jnp
from jax import lax
from jax.experimental import pallas as pl
from jax.experimental.pallas import tpu as pltpu
from jax.sharding import Mesh, PartitionSpec as P

BLK = 128
NZ, NX, NCORE = 8, 4, 2
LEVELS = (5, 6, 8)
BF = jnp.bfloat16
VMEM = pl.BlockSpec(memory_space=pltpu.VMEM)
ANY = pl.BlockSpec(memory_space=pl.ANY)
SMEM = pl.BlockSpec(memory_space=pltpu.SMEM)


def params(mib):
    return pltpu.CompilerParams(vmem_limit_bytes=mib << 20)


def cost(nbytes, flops=0):
    return pl.CostEstimate(flops=flops, bytes_accessed=nbytes, transcendentals=0)


def turn(start, k, n):
    at = start + k
    at = jnp.where(at >= n, at - n, at)
    return jnp.where(at < 0, at + n, at)


def coef_pick_kernel(me, rows, coef, after, *outs):
    slots = outs[0].shape[0]
    for k, out in enumerate(outs):
        base = turn(me[0], k, len(outs)) * slots

        def step(t, _):
            start = pl.multiple_of(rows[base + t] * BLK, BLK)
            out[t] = coef[:, pl.ds(start, BLK)]
            return 0

        lax.fori_loop(0, slots, step, 0, unroll=4)


def coef_pick(me, coef_t, rows, after, groups):
    slots, occ = rows.shape[0] // groups, coef_t.shape[0]
    return pl.pallas_call(
        coef_pick_kernel,
        out_shape=[jax.ShapeDtypeStruct((slots, occ, BLK), BF)] * groups,
        in_specs=[SMEM, SMEM, VMEM, ANY],
        out_specs=[VMEM] * groups,
        compiler_params=params(16),
        cost_estimate=cost(4 << 20),
        name="coef_pick",
    )(me, rows, coef_t, after)


def coef_join_kernel(me, pos, *rest):
    pieces, out, held = rest[:-2], rest[-2], rest[-1]
    groups, owned = len(pieces), out.shape[0]
    for k, piece in enumerate(pieces):
        held[turn(me[0], -k, groups)] = piece[...]

    def step(k, _):
        parts = []
        for s in range(groups):
            p = pos[s * owned + k]
            block = held[s, jnp.maximum(p, 0)]
            parts.append(jnp.where(p >= 0, block, jnp.zeros_like(block)))
        out[k] = jnp.concatenate(parts, axis=0).T
        return 0

    lax.fori_loop(0, owned, step, 0)


def coef_join(me, pieces, pos, owned):
    groups = len(pieces)
    slots, occ, _ = pieces[0].shape
    return pl.pallas_call(
        coef_join_kernel,
        out_shape=jax.ShapeDtypeStruct((owned, BLK, groups * occ), BF),
        in_specs=[SMEM, SMEM] + [VMEM] * groups,
        out_specs=VMEM,
        scratch_shapes=[pltpu.VMEM((groups, slots, occ, BLK), BF)],
        compiler_params=params(16),
        cost_estimate=cost(4 << 20),
        name="coef_join",
    )(me, pos, *pieces)


def core_split_kernel(batch, at, pairs, *rest):
    outs, sems = rest[:-1], rest[-1]
    copies = []
    for k, out in enumerate(outs):
        core = at[1] if k == 0 else 1 - at[1]
        copies.append(pltpu.make_async_copy(pairs.at[batch, :, :, core], out, sems.at[k]))
    for copy in copies:
        copy.start()
    for copy in copies:
        copy.wait()


def core_split(batch, at, pairs):
    _, nz, nx, _, occ, width = pairs.shape
    return pl.pallas_call(
        functools.partial(core_split_kernel, batch),
        out_shape=[jax.ShapeDtypeStruct((nz, nx, occ, width), BF)] * 2,
        in_specs=[SMEM, pl.BlockSpec(memory_space=pltpu.HBM)],
        out_specs=[VMEM] * 2,
        scratch_shapes=[pltpu.SemaphoreType.DMA((2,))],
        compiler_params=params(12),
        cost_estimate=cost(4 << 20),
        name=f"core_split{batch}",
    )(at, pairs)


def cut_tile(odd, t, left, right, out, j):
    rows, occ, width = left.shape
    lo = t * BLK - (BLK // 2 if odd else 0)
    first, last = max(lo, 0), min(lo + BLK, 2 * width)

    def row(i, _):
        parts = []
        if lo < 0:
            parts.append(jnp.zeros((occ, -lo), BF))
        if first < width:
            parts.append(left[i, :, first : min(last, width)])
        if last > width:
            parts.append(right[i, :, max(first, width) - width : last - width])
        if last < lo + BLK:
            parts.append(jnp.zeros((occ, lo + BLK - last), BF))
        to = i % NX * NZ + i // NX
        out[to, j] = parts[0] if len(parts) == 1 else jnp.concatenate(parts, axis=1)
        return 0

    lax.fori_loop(0, rows, row, 0)


def tile_pick_kernel(at, listed, own, got, after, out):
    held = listed.shape[0] - 1
    for odd in (0, 1):
        for core in (0, 1):
            left, right = (own, got) if core == 0 else (got, own)

            @pl.when((at[0] % 2 == odd) & (at[1] == core))
            def _():
                def keep(j, _):
                    for t in range(held):

                        @pl.when(listed[j] == t)
                        def _():
                            cut_tile(odd, t, left, right, out, j)

                    return 0

                lax.fori_loop(0, jnp.minimum(listed[held], out.shape[1]), keep, 0)


def tile_pick(at, listed, own, got, after, cap):
    rows, occ, width = own.shape
    return pl.pallas_call(
        tile_pick_kernel,
        out_shape=jax.ShapeDtypeStruct((rows, cap, occ, BLK), BF),
        in_specs=[SMEM, SMEM, VMEM, VMEM, ANY],
        out_specs=VMEM,
        compiler_params=params(16),
        cost_estimate=cost(4 << 20),
        name="tile_pick",
    )(at, listed, own, got, after)


def slot_pick_kernel(me, spots, got, *outs):
    slots, occ, _ = outs[0].shape
    low = lax.broadcasted_iota(jnp.int32, (occ, BLK), 1) < BLK // 2
    total = len(outs) * slots
    for k, out in enumerate(outs):
        base = turn(me[0], k, len(outs)) * slots

        def step(t, _):
            a, b = spots[base + t], spots[total + base + t]
            out[t] = jnp.where(low, got[a >> 3, a & 7], got[b >> 3, b & 7])
            return 0

        lax.fori_loop(0, slots, step, 0, unroll=5)


def slot_pick(me, spots, got, groups):
    slots = spots.shape[0] // (2 * groups)
    occ = got.shape[2]
    return pl.pallas_call(
        slot_pick_kernel,
        out_shape=[jax.ShapeDtypeStruct((slots, occ, BLK), BF)] * groups,
        in_specs=[SMEM, SMEM, VMEM],
        out_specs=[VMEM] * groups,
        compiler_params=params(16),
        cost_estimate=cost(2 << 20),
        name="slot_pick",
    )(me, spots, got)


def product_kernel(per, groups, me, pos, coef, *rest):
    gamma, (out, held) = rest[:groups], rest[-2:]
    owned = pos.shape[0] // groups
    step = pl.program_id(0)

    @pl.when(step == 0)
    def _():
        for k in range(groups):
            held[turn(me[0], -k, groups)] = gamma[k][...]

    for j in range(per):
        at = [jnp.maximum(pos[s * owned + step * per + j], 0) for s in range(groups)]
        cols = jnp.concatenate([held[s, at[s]] for s in range(groups)], axis=0)
        total = jnp.dot(coef[j], cols, preferred_element_type=jnp.float32)
        out[0, 0, j] = total.astype(BF)


def product(batch, batches, me, coef, gamma, pos, prior):
    owned = coef.shape[0]
    groups = len(gamma)
    per = 20
    extra = [] if prior is None else [prior]
    return pl.pallas_call(
        functools.partial(product_kernel, per, groups),
        out_shape=jax.ShapeDtypeStruct((batches, 1, owned, BLK, BLK), BF),
        grid_spec=pltpu.PrefetchScalarGridSpec(
            num_scalar_prefetch=2,
            grid=(owned // per,),
            in_specs=[pl.BlockSpec((per, BLK, coef.shape[2]), lambda i, *_: (i, 0, 0))]
            + [pl.BlockSpec(gamma[0].shape, lambda i, *_: (0, 0, 0))] * groups
            + [ANY] * len(extra),
            out_specs=pl.BlockSpec((1, 1, per, BLK, BLK), lambda i, *_: (batch, 0, i, 0, 0)),
            scratch_shapes=[pltpu.VMEM((groups,) + gamma[0].shape, BF)],
        ),
        input_output_aliases={3 + groups: 0} if extra else {},
        compiler_params=params(16),
        cost_estimate=cost(6 << 20, 2 * owned * BLK**3),
        name=f"product{batch}",
    )(me, pos, coef, *gamma, *extra)


def local(gamma_pairs, occ_coef, block_lists, block_counts, block_coords):
    batches, aux, occ, width = gamma_pairs.shape
    groups = lax.axis_size("sp")
    basis = occ_coef.shape[0]
    nblk = basis // BLK
    total_blocks = block_coords.shape[0]
    owned = total_blocks // groups
    capacity = block_lists.shape[2]
    me_s = lax.axis_index("sp")
    me_z = lax.axis_index("z")

    at = jnp.stack([lax.axis_index("x"), lax.axis_index("core")]).astype(jnp.int32)
    pairs = gamma_pairs.reshape(batches, NZ, NX, NCORE, occ, width)

    pairs = pltpu.with_memory_space_constraint(pairs, pltpu.HBM)

    def swap(halves):
        return halves[0], lax.ppermute(halves[1], "core", [(0, 1), (1, 0)])

    split0, block_lists, block_counts, block_coords = lax.optimization_barrier(
        (core_split(0, at, pairs), block_lists, block_counts, block_coords)
    )
    halves0 = swap(split0)

    valid = jnp.arange(capacity, dtype=jnp.int32)[None, None, :] < block_counts[:, :, None]
    lists = jnp.clip(block_lists, 0, owned - 1)
    ids = lists + (jnp.arange(groups, dtype=jnp.int32) * owned)[None, :, None]
    hit = ids.reshape(groups, -1, 1) == jnp.arange(total_blocks, dtype=jnp.int32)
    row_ids = jnp.sum(jnp.where(hit, block_coords[:, 0], 0), axis=2)
    col_ids = jnp.sum(jnp.where(hit, block_coords[:, 1], 0), axis=2)
    live_col = jnp.where(valid.reshape(groups, -1), col_ids, -1)
    need = jnp.any(live_col[:, :, None] == jnp.arange(nblk, dtype=jnp.int32), axis=1)
    pair_blocks = 2 * nblk // (NZ * NX)
    held = -(-2 * width // BLK)
    need = need.reshape(groups, NZ * NX // 2, 1, pair_blocks).astype(jnp.int32)
    need = jnp.concatenate([need[..., :held], need[..., pair_blocks - held :]], axis=2)
    need = need.reshape(groups, NZ * NX, held)
    most = jnp.max(jnp.sum(need, axis=2))
    my_need = lax.dynamic_index_in_dim(need, me_s, 0, keepdims=False)
    tile_ids = jnp.arange(held, dtype=jnp.int32)
    before = (tile_ids[None, :] < tile_ids[:, None]).astype(jnp.int32)
    rank = jnp.sum(my_need[:, None, :] * before[None], axis=2)
    my_cols = lax.dynamic_index_in_dim(col_ids, me_s, 0, keepdims=False)
    my_rows = lax.dynamic_index_in_dim(row_ids, me_s, 0, keepdims=False)
    my_live = lax.dynamic_index_in_dim(valid.reshape(groups, -1), me_s, 0, keepdims=False)
    slot_cols = my_cols.reshape(groups, capacity)
    slot_cols = jnp.where(my_live.reshape(groups, capacity), slot_cols, slot_cols[:, :1])
    slot_cols = slot_cols.reshape(-1)
    two_chips, within = slot_cols // pair_blocks, slot_cols % pair_blocks
    upper = jnp.arange(2, dtype=jnp.int32)[:, None]
    on_odd = (within[None, :] > held - 1 - upper).astype(jnp.int32)
    chip = 2 * two_chips[None, :] + on_odd
    tile = within[None, :] - on_odd * (pair_blocks - held)
    tile_hit = (chip * held + tile)[:, :, None] == jnp.arange(NZ * NX * held, dtype=jnp.int32)
    order = jnp.sum(jnp.where(tile_hit, rank.reshape(-1), 0), axis=2)
    spots = (8 * (chip % NX * NZ + chip // NX) + order).reshape(-1)
    my_chip = me_z * NX + lax.axis_index("x")
    chip_need = lax.dynamic_index_in_dim(my_need, my_chip, 0, keepdims=False)
    chip_rank = lax.dynamic_index_in_dim(rank, my_chip, 0, keepdims=False)
    listed = jnp.sum(
        jnp.where(
            (chip_rank[None, :] == tile_ids[:, None]) & (chip_need[None, :] > 0),
            tile_ids[None, :],
            0,
        ),
        axis=1,
    )
    listed = jnp.concatenate([listed, jnp.sum(chip_need, keepdims=True)])
    to_me = lax.dynamic_index_in_dim(lists, me_s, 1, keepdims=False)
    to_me_valid = lax.dynamic_index_in_dim(valid, me_s, 1, keepdims=False)
    hits = (to_me[:, None, :] == jnp.arange(owned, dtype=jnp.int32)[None, :, None]) & to_me_valid[
        :, None, :
    ]
    slot_no = jnp.arange(capacity, dtype=jnp.int32) + 1
    pos = (jnp.sum(jnp.where(hits, slot_no, 0), axis=2) - 1).reshape(-1)

    me = me_s[None].astype(jnp.int32)
    def exchange_owners(sent):
        return [sent[0]] + [
            lax.ppermute(sent[k], "sp", [(i, (i + k) % groups) for i in range(groups)])
            for k in range(1, groups)
        ]

    def finish(cap, halves0, pairs, coef_t, my_rows, pos, listed, spots):
        def tiles(halves, after):
            halves = [half.reshape(NZ * NX, occ, width) for half in halves]
            picked = tile_pick(at, listed, *halves, after, cap)
            return picked, lax.all_to_all(picked, ("x", "z"), 0, 0, tiled=True)

        def owners(got):
            return exchange_owners(slot_pick(me, spots, got, groups))

        picked0, got0 = tiles(halves0, me)
        coef_parts = exchange_owners(coef_pick(me, coef_t, my_rows, picked0, groups))
        coef = coef_join(me, coef_parts, pos, owned)
        _, got1 = tiles(swap(core_split(1, at, pairs)), coef)
        out = product(0, batches, me, coef, owners(got0), pos, None)
        return product(1, batches, me, coef, owners(got1), pos, out)

    level = sum((most > cap).astype(jnp.int32) for cap in LEVELS[:-1])
    level, *tables = lax.optimization_barrier((level, my_rows, pos, listed, spots))
    branches = [functools.partial(finish, cap) for cap in LEVELS]
    return lax.switch(level, branches, halves0, pairs, occ_coef.T, *tables)


def solution(mesh):
    groups = mesh.shape["sp"]
    grid = Mesh(mesh.devices.reshape(NZ, NX, NCORE, groups), ("z", "x", "core", "sp"))
    pair = ("z", "x", "core")
    in_specs = (P(None, None, "sp", pair), P(None, "sp"), P(), P(), P())
    out_specs = P(None, pair, "sp", None, None)
    return jax.shard_map(local, mesh=grid, in_specs=in_specs, out_specs=out_specs, check_vma=False)
```

```python
import functools

import jax
import jax.numpy as jnp
from jax import lax
from jax.experimental import pallas as pl
from jax.experimental.pallas import tpu as pltpu
from jax.sharding import Mesh, PartitionSpec as P

BLK = 128
NZ, NX, NCORE = 8, 4, 2
LEVELS = (5, 6, 8)
BF = jnp.bfloat16
VMEM = pl.BlockSpec(memory_space=pltpu.VMEM)
ANY = pl.BlockSpec(memory_space=pl.ANY)
SMEM = pl.BlockSpec(memory_space=pltpu.SMEM)


def params(mib):
    return pltpu.CompilerParams(vmem_limit_bytes=mib << 20)


def cost(nbytes, flops=0):
    return pl.CostEstimate(flops=flops, bytes_accessed=nbytes, transcendentals=0)


def turn(start, k, n):
    at = start + k
    at = jnp.where(at >= n, at - n, at)
    return jnp.where(at < 0, at + n, at)


def coef_pick_kernel(me, rows, coef, after, *outs):
    slots = outs[0].shape[0]
    for k, out in enumerate(outs):
        base = turn(me[0], k, len(outs)) * slots

        def step(t, _):
            start = pl.multiple_of(rows[base + t] * BLK, BLK)
            out[t] = coef[:, pl.ds(start, BLK)]
            return 0

        lax.fori_loop(0, slots, step, 0, unroll=4)


def coef_pick(me, coef_t, rows, after, groups):
    slots, occ = rows.shape[0] // groups, coef_t.shape[0]
    return pl.pallas_call(
        coef_pick_kernel,
        out_shape=[jax.ShapeDtypeStruct((slots, occ, BLK), BF)] * groups,
        in_specs=[SMEM, SMEM, VMEM, ANY],
        out_specs=[VMEM] * groups,
        compiler_params=params(16),
        cost_estimate=cost(4 << 20),
        name="coef_pick",
    )(me, rows, coef_t, after)


def coef_join_kernel(me, pos, *rest):
    pieces, out, held = rest[:-2], rest[-2], rest[-1]
    groups, owned = len(pieces), out.shape[0]
    for k, piece in enumerate(pieces):
        held[turn(me[0], -k, groups)] = piece[...]

    def step(k, _):
        parts = []
        for s in range(groups):
            p = pos[s * owned + k]
            block = held[s, jnp.maximum(p, 0)]
            parts.append(jnp.where(p >= 0, block, jnp.zeros_like(block)))
        out[k] = jnp.concatenate(parts, axis=0).T
        return 0

    lax.fori_loop(0, owned, step, 0)


def coef_join(me, pieces, pos, owned):
    groups = len(pieces)
    slots, occ, _ = pieces[0].shape
    return pl.pallas_call(
        coef_join_kernel,
        out_shape=jax.ShapeDtypeStruct((owned, BLK, groups * occ), BF),
        in_specs=[SMEM, SMEM] + [VMEM] * groups,
        out_specs=VMEM,
        scratch_shapes=[pltpu.VMEM((groups, slots, occ, BLK), BF)],
        compiler_params=params(16),
        cost_estimate=cost(4 << 20),
        name="coef_join",
    )(me, pos, *pieces)


def core_split_kernel(batch, at, pairs, *rest):
    outs, sems = rest[:-1], rest[-1]
    copies = []
    for k, out in enumerate(outs):
        core = at[1] if k == 0 else 1 - at[1]
        copies.append(pltpu.make_async_copy(pairs.at[batch, :, :, core], out, sems.at[k]))
    for copy in copies:
        copy.start()
    for copy in copies:
        copy.wait()


def core_split(batch, at, pairs):
    _, nz, nx, _, occ, width = pairs.shape
    return pl.pallas_call(
        functools.partial(core_split_kernel, batch),
        out_shape=[jax.ShapeDtypeStruct((nz, nx, occ, width), BF)] * 2,
        in_specs=[SMEM, pl.BlockSpec(memory_space=pltpu.HBM)],
        out_specs=[VMEM] * 2,
        scratch_shapes=[pltpu.SemaphoreType.DMA((2,))],
        compiler_params=params(12),
        cost_estimate=cost(4 << 20),
        name=f"core_split{batch}",
    )(at, pairs)


def tile_pick_kernel(at, listed, own, got, after, out, token):
    rows, occ, width = own.shape
    token[0] = at[0]
    half = BLK // 2 * (at[0] % 2)
    source = lax.broadcasted_iota(jnp.int32, (width, BLK), 0)
    column = lax.broadcasted_iota(jnp.int32, (width, BLK), 1)
    per = 8

    def keep(j, _):
        start = listed[j] * BLK - half
        own_from, got_from = width * at[1], width * (1 - at[1])

        def overlaps(base):
            return (start < base + width) & (start + BLK > base)

        def move(*parts):
            picks = [(ref, (source == column + (start - base)).astype(BF)) for ref, base in parts]

            def some(i, _):
                total = sum(
                    jnp.dot(
                        ref[pl.ds(i * per, per)].reshape(per * occ, width),
                        pick,
                        preferred_element_type=jnp.float32,
                    )
                    for ref, pick in picks
                )
                out[pl.ds(i * per, per), j] = total.astype(BF).reshape(per, occ, BLK)
                return 0

            lax.fori_loop(0, rows // per, some, 0, unroll=1)

        in_own, in_got = overlaps(own_from), overlaps(got_from)
        pl.when(in_own & in_got)(lambda: move((own, own_from), (got, got_from)))
        pl.when(in_own & jnp.logical_not(in_got))(lambda: move((own, own_from)))
        pl.when(in_got & jnp.logical_not(in_own))(lambda: move((got, got_from)))
        return 0

    held = listed.shape[0] - 1
    lax.fori_loop(0, jnp.minimum(listed[held], out.shape[1]), keep, 0)


def tile_pick(at, listed, own, got, after, cap):
    rows, occ, width = own.shape
    return pl.pallas_call(
        tile_pick_kernel,
        out_shape=[
            jax.ShapeDtypeStruct((rows, cap, occ, BLK), BF),
            jax.ShapeDtypeStruct((1,), jnp.int32),
        ],
        in_specs=[SMEM, SMEM, VMEM, VMEM, ANY],
        out_specs=[VMEM, SMEM],
        compiler_params=params(16),
        cost_estimate=cost(4 << 20),
        name="tile_pick",
    )(at, listed, own, got, after)


def slot_pick_kernel(me, spots, got, *outs):
    slots, occ, _ = outs[0].shape
    low = lax.broadcasted_iota(jnp.int32, (occ, BLK), 1) < BLK // 2
    total = len(outs) * slots
    for k, out in enumerate(outs):
        base = turn(me[0], k, len(outs)) * slots

        def step(t, _):
            a, b = spots[base + t], spots[total + base + t]
            out[t] = jnp.where(low, got[a >> 3, a & 7], got[b >> 3, b & 7])
            return 0

        lax.fori_loop(0, slots, step, 0, unroll=4)


def slot_pick(me, spots, got, groups):
    slots = spots.shape[0] // (2 * groups)
    occ = got.shape[2]
    return pl.pallas_call(
        slot_pick_kernel,
        out_shape=[jax.ShapeDtypeStruct((slots, occ, BLK), BF)] * groups,
        in_specs=[SMEM, SMEM, VMEM],
        out_specs=[VMEM] * groups,
        compiler_params=params(16),
        cost_estimate=cost(2 << 20),
        name="slot_pick",
    )(me, spots, got)


def product_kernel(per, groups, me, pos, coef, *rest):
    gamma, (out, held) = rest[:groups], rest[-2:]
    owned = pos.shape[0] // groups
    step = pl.program_id(0)

    @pl.when(step == 0)
    def _():
        for k in range(groups):
            held[turn(me[0], -k, groups)] = gamma[k][...]

    for j in range(per):
        at = [jnp.maximum(pos[s * owned + step * per + j], 0) for s in range(groups)]
        cols = jnp.concatenate([held[s, at[s]] for s in range(groups)], axis=0)
        total = jnp.dot(coef[j], cols, preferred_element_type=jnp.float32)
        out[0, 0, j] = total.astype(BF)


def product(batch, batches, me, coef, gamma, pos, prior):
    owned = coef.shape[0]
    groups = len(gamma)
    per = 20
    extra = [] if prior is None else [prior]
    return pl.pallas_call(
        functools.partial(product_kernel, per, groups),
        out_shape=jax.ShapeDtypeStruct((batches, 1, owned, BLK, BLK), BF),
        grid_spec=pltpu.PrefetchScalarGridSpec(
            num_scalar_prefetch=2,
            grid=(owned // per,),
            in_specs=[pl.BlockSpec((per, BLK, coef.shape[2]), lambda i, *_: (i, 0, 0))]
            + [pl.BlockSpec(gamma[0].shape, lambda i, *_: (0, 0, 0))] * groups
            + [ANY] * len(extra),
            out_specs=pl.BlockSpec((1, 1, per, BLK, BLK), lambda i, *_: (batch, 0, i, 0, 0)),
            scratch_shapes=[pltpu.VMEM((groups,) + gamma[0].shape, BF)],
        ),
        input_output_aliases={3 + groups: 0} if extra else {},
        compiler_params=params(16),
        cost_estimate=cost(6 << 20, 2 * owned * BLK**3),
        name=f"product{batch}",
    )(me, pos, coef, *gamma, *extra)


def local(gamma_pairs, occ_coef, block_lists, block_counts, block_coords):
    batches, aux, occ, width = gamma_pairs.shape
    groups = lax.axis_size("sp")
    basis = occ_coef.shape[0]
    nblk = basis // BLK
    total_blocks = block_coords.shape[0]
    owned = total_blocks // groups
    capacity = block_lists.shape[2]
    me_s = lax.axis_index("sp")
    me_z = lax.axis_index("z")

    at = jnp.stack([lax.axis_index("x"), lax.axis_index("core")]).astype(jnp.int32)
    pairs = gamma_pairs.reshape(batches, NZ, NX, NCORE, occ, width)

    pairs = pltpu.with_memory_space_constraint(pairs, pltpu.HBM)

    def swap(halves):
        return halves[0], lax.ppermute(halves[1], "core", [(0, 1), (1, 0)])

    split0, block_lists, block_counts, block_coords = lax.optimization_barrier(
        (core_split(0, at, pairs), block_lists, block_counts, block_coords)
    )
    halves0 = swap(split0)

    valid = jnp.arange(capacity, dtype=jnp.int32)[None, None, :] < block_counts[:, :, None]
    lists = jnp.clip(block_lists, 0, owned - 1)
    ids = lists + (jnp.arange(groups, dtype=jnp.int32) * owned)[None, :, None]
    hit = ids.reshape(groups, -1, 1) == jnp.arange(total_blocks, dtype=jnp.int32)
    row_ids = jnp.sum(jnp.where(hit, block_coords[:, 0], 0), axis=2)
    col_ids = jnp.sum(jnp.where(hit, block_coords[:, 1], 0), axis=2)
    live_col = jnp.where(valid.reshape(groups, -1), col_ids, -1)
    need = jnp.any(live_col[:, :, None] == jnp.arange(nblk, dtype=jnp.int32), axis=1)
    pair_blocks = 2 * nblk // (NZ * NX)
    held = -(-2 * width // BLK)
    need = need.reshape(groups, NZ * NX // 2, 1, pair_blocks).astype(jnp.int32)
    need = jnp.concatenate([need[..., :held], need[..., pair_blocks - held :]], axis=2)
    need = need.reshape(groups, NZ * NX, held)
    most = jnp.max(jnp.sum(need, axis=2))
    my_need = lax.dynamic_index_in_dim(need, me_s, 0, keepdims=False)
    tile_ids = jnp.arange(held, dtype=jnp.int32)
    before = (tile_ids[None, :] < tile_ids[:, None]).astype(jnp.int32)
    rank = jnp.sum(my_need[:, None, :] * before[None], axis=2)
    my_cols = lax.dynamic_index_in_dim(col_ids, me_s, 0, keepdims=False)
    my_chip = me_z * NX + lax.axis_index("x")
    chip_need = lax.dynamic_index_in_dim(my_need, my_chip, 0, keepdims=False)
    chip_rank = lax.dynamic_index_in_dim(rank, my_chip, 0, keepdims=False)
    listed = jnp.sum(
        jnp.where(
            (chip_rank[None, :] == tile_ids[:, None]) & (chip_need[None, :] > 0),
            tile_ids[None, :],
            0,
        ),
        axis=1,
    )
    listed = jnp.concatenate([listed, jnp.sum(chip_need, keepdims=True)])
    me = jnp.stack([me_s, me_z]).astype(jnp.int32)

    def exchange_owners(sent):
        return [sent[0]] + [
            lax.ppermute(sent[k], "sp", [(i, (i + k) % groups) for i in range(groups)])
            for k in range(1, groups)
        ]

    def tables(lists, valid, row_ids, my_cols, rank):
        my_live = lax.dynamic_index_in_dim(valid.reshape(groups, -1), me_s, 0, keepdims=False)
        my_rows = lax.dynamic_index_in_dim(row_ids, me_s, 0, keepdims=False)
        slot_cols = my_cols.reshape(groups, capacity)
        slot_cols = jnp.where(my_live.reshape(groups, capacity), slot_cols, slot_cols[:, :1])
        slot_cols = slot_cols.reshape(-1)
        two_chips, within = slot_cols // pair_blocks, slot_cols % pair_blocks
        upper = jnp.arange(2, dtype=jnp.int32)[:, None]
        on_odd = (within[None, :] > held - 1 - upper).astype(jnp.int32)
        chip = 2 * two_chips[None, :] + on_odd
        tile = within[None, :] - on_odd * (pair_blocks - held)
        tile_hit = (chip * held + tile)[:, :, None] == jnp.arange(NZ * NX * held, dtype=jnp.int32)
        order = jnp.sum(jnp.where(tile_hit, rank.reshape(-1), 0), axis=2)
        spots = (8 * chip + order).reshape(-1)
        to_me = lax.dynamic_index_in_dim(lists, me_s, 1, keepdims=False)
        to_me_valid = lax.dynamic_index_in_dim(valid, me_s, 1, keepdims=False)
        hits = (to_me[:, None, :] == jnp.arange(owned, dtype=jnp.int32)[None, :, None]) & to_me_valid[
            :, None, :
        ]
        slot_no = jnp.arange(capacity, dtype=jnp.int32) + 1
        pos = (jnp.sum(jnp.where(hits, slot_no, 0), axis=2) - 1).reshape(-1)

        return my_rows, pos, spots

    def finish(cap, halves0, pairs, coef_t, listed, *lookups):
        def tiles(halves, after):
            halves = [half.reshape(NZ * NX, occ, width) for half in halves]
            picked, token = tile_pick(at, listed, *halves, after, cap)
            return token, lax.all_to_all(picked, ("z", "x"), 0, 0, tiled=True)

        def owners(got):
            return exchange_owners(slot_pick(me, spots, got, groups))

        token, got0 = tiles(halves0, me)
        *lookups, token = lax.optimization_barrier((*lookups, token))
        my_rows, pos, spots = tables(*lookups)
        coef_parts = exchange_owners(coef_pick(me, coef_t, my_rows, token, groups))
        coef = coef_join(me, coef_parts, pos, owned)
        _, got1 = tiles(swap(core_split(1, at, pairs)), coef)
        out = product(0, batches, me, coef, owners(got0), pos, None)
        return product(1, batches, me, coef, owners(got1), pos, out)

    level = sum((most > cap).astype(jnp.int32) for cap in LEVELS[:-1])
    level, listed = lax.optimization_barrier((level, listed))
    lookups = (lists, valid, row_ids, my_cols, rank)
    branches = [functools.partial(finish, cap) for cap in LEVELS]
    return lax.switch(level, branches, halves0, pairs, occ_coef.T, listed, *lookups)


def solution(mesh):
    groups = mesh.shape["sp"]
    grid = Mesh(mesh.devices.reshape(NZ, NX, NCORE, groups), ("z", "x", "core", "sp"))
    pair = ("z", "x", "core")
    in_specs = (P(None, None, "sp", pair), P(None, "sp"), P(), P(), P())
    out_specs = P(None, pair, "sp", None, None)
    return jax.shard_map(local, mesh=grid, in_specs=in_specs, out_specs=out_specs, check_vma=False)
```

```python
import functools

import jax
import jax.numpy as jnp
from jax import lax
from jax.experimental import pallas as pl
from jax.experimental.pallas import tpu as pltpu
from jax.sharding import Mesh, PartitionSpec as P

BLK = 128
NZ, NX, NCORE = 8, 4, 2
LEVELS = (5, 6, 8)
BF = jnp.bfloat16
VMEM = pl.BlockSpec(memory_space=pltpu.VMEM)
ANY = pl.BlockSpec(memory_space=pl.ANY)
SMEM = pl.BlockSpec(memory_space=pltpu.SMEM)


def params(mib):
    return pltpu.CompilerParams(vmem_limit_bytes=mib << 20)


def cost(nbytes, flops=0):
    return pl.CostEstimate(flops=flops, bytes_accessed=nbytes, transcendentals=0)


def turn(start, k, n):
    at = start + k
    at = jnp.where(at >= n, at - n, at)
    return jnp.where(at < 0, at + n, at)


def coef_pick_kernel(me, rows, coef, after, *outs):
    slots = outs[0].shape[0]
    for k, out in enumerate(outs):
        base = turn(me[0], k, len(outs)) * slots

        def step(t, _):
            start = pl.multiple_of(rows[base + t] * BLK, BLK)
            out[t] = coef[:, pl.ds(start, BLK)]
            return 0

        lax.fori_loop(0, slots, step, 0, unroll=4)


def coef_pick(me, coef_t, rows, after, groups):
    slots, occ = rows.shape[0] // groups, coef_t.shape[0]
    return pl.pallas_call(
        coef_pick_kernel,
        out_shape=[jax.ShapeDtypeStruct((slots, occ, BLK), BF)] * groups,
        in_specs=[SMEM, SMEM, VMEM, ANY],
        out_specs=[VMEM] * groups,
        compiler_params=params(16),
        cost_estimate=cost(4 << 20),
        name="coef_pick",
    )(me, rows, coef_t, after)


def coef_join_kernel(me, pos, *rest):
    pieces, out, held = rest[:-2], rest[-2], rest[-1]
    groups, owned = len(pieces), out.shape[0]
    for k, piece in enumerate(pieces):
        held[turn(me[0], -k, groups)] = piece[...]

    def step(k, _):
        parts = []
        for s in range(groups):
            p = pos[s * owned + k]
            block = held[s, jnp.maximum(p, 0)]
            parts.append(jnp.where(p >= 0, block, jnp.zeros_like(block)))
        out[k] = jnp.concatenate(parts, axis=0).T
        return 0

    lax.fori_loop(0, owned, step, 0)


def coef_join(me, pieces, pos, owned):
    groups = len(pieces)
    slots, occ, _ = pieces[0].shape
    return pl.pallas_call(
        coef_join_kernel,
        out_shape=jax.ShapeDtypeStruct((owned, BLK, groups * occ), BF),
        in_specs=[SMEM, SMEM] + [VMEM] * groups,
        out_specs=VMEM,
        scratch_shapes=[pltpu.VMEM((groups, slots, occ, BLK), BF)],
        compiler_params=params(16),
        cost_estimate=cost(4 << 20),
        name="coef_join",
    )(me, pos, *pieces)


def core_split_kernel(batch, at, pairs, *rest):
    outs, sems = rest[:-1], rest[-1]
    copies = []
    for k, out in enumerate(outs):
        core = at[1] if k == 0 else 1 - at[1]
        copies.append(pltpu.make_async_copy(pairs.at[batch, :, :, core], out, sems.at[k]))
    for copy in copies:
        copy.start()
    for copy in copies:
        copy.wait()


def core_split(batch, at, pairs):
    _, nz, nx, _, occ, width = pairs.shape
    return pl.pallas_call(
        functools.partial(core_split_kernel, batch),
        out_shape=[jax.ShapeDtypeStruct((nz, nx, occ, width), BF)] * 2,
        in_specs=[SMEM, pl.BlockSpec(memory_space=pltpu.HBM)],
        out_specs=[VMEM] * 2,
        scratch_shapes=[pltpu.SemaphoreType.DMA((2,))],
        compiler_params=params(12),
        cost_estimate=cost(4 << 20),
        name=f"core_split{batch}",
    )(at, pairs)


def tile_pick_kernel(at, listed, own, got, after, out, token):
    rows, occ, width = own.shape
    token[0] = at[0]
    half = BLK // 2 * (at[0] % 2)
    source = lax.broadcasted_iota(jnp.int32, (width, BLK), 0)
    column = lax.broadcasted_iota(jnp.int32, (width, BLK), 1)
    per = 8

    def keep(j, _):
        start = listed[j] * BLK - half
        own_from, got_from = width * at[1], width * (1 - at[1])

        def overlaps(base):
            return (start < base + width) & (start + BLK > base)

        def move(*parts):
            picks = [(ref, (source == column + (start - base)).astype(BF)) for ref, base in parts]

            def some(i, _):
                total = sum(
                    jnp.dot(
                        ref[pl.ds(i * per, per)].reshape(per * occ, width),
                        pick,
                        preferred_element_type=jnp.float32,
                    )
                    for ref, pick in picks
                )
                out[pl.ds(i * per, per), j] = total.astype(BF).reshape(per, occ, BLK)
                return 0

            lax.fori_loop(0, rows // per, some, 0, unroll=1)

        in_own, in_got = overlaps(own_from), overlaps(got_from)
        pl.when(in_own & in_got)(lambda: move((own, own_from), (got, got_from)))
        pl.when(in_own & jnp.logical_not(in_got))(lambda: move((own, own_from)))
        pl.when(in_got & jnp.logical_not(in_own))(lambda: move((got, got_from)))
        return 0

    held = listed.shape[0] - 1
    lax.fori_loop(0, jnp.minimum(listed[held], out.shape[1]), keep, 0)


def tile_pick(at, listed, own, got, after, cap):
    rows, occ, width = own.shape
    return pl.pallas_call(
        tile_pick_kernel,
        out_shape=[
            jax.ShapeDtypeStruct((rows, cap, occ, BLK), BF),
            jax.ShapeDtypeStruct((1,), jnp.int32),
        ],
        in_specs=[SMEM, SMEM, VMEM, VMEM, ANY],
        out_specs=[VMEM, SMEM],
        compiler_params=params(16),
        cost_estimate=cost(4 << 20),
        name="tile_pick",
    )(at, listed, own, got, after)


def slot_pick_kernel(me, spots, got, after, *outs):
    slots, occ, _ = outs[0].shape
    low = lax.broadcasted_iota(jnp.int32, (occ, BLK), 1) < BLK // 2
    total = len(outs) * slots
    for k, out in enumerate(outs):
        base = turn(me[0], k, len(outs)) * slots

        def step(t, _):
            a, b = spots[base + t], spots[total + base + t]
            out[t] = jnp.where(low, got[a >> 3, a & 7], got[b >> 3, b & 7])
            return 0

        lax.fori_loop(0, slots, step, 0, unroll=4)


def slot_pick(me, spots, got, after, groups):
    slots = spots.shape[0] // (2 * groups)
    occ = got.shape[2]
    return pl.pallas_call(
        slot_pick_kernel,
        out_shape=[jax.ShapeDtypeStruct((slots, occ, BLK), BF)] * groups,
        in_specs=[SMEM, SMEM, VMEM, ANY],
        out_specs=[VMEM] * groups,
        compiler_params=params(16),
        cost_estimate=cost(2 << 20),
        name="slot_pick",
    )(me, spots, got, after)


def product_kernel(per, groups, me, pos, coef, *rest):
    gamma, (out, token, held) = rest[:groups], rest[-3:]
    token[0] = me[0]
    owned = pos.shape[0] // groups
    step = pl.program_id(0)

    @pl.when(step == 0)
    def _():
        for k in range(groups):
            held[turn(me[0], -k, groups)] = gamma[k][...]

    for j in range(per):
        at = [jnp.maximum(pos[s * owned + step * per + j], 0) for s in range(groups)]
        cols = jnp.concatenate([held[s, at[s]] for s in range(groups)], axis=0)
        total = jnp.dot(coef[j], cols, preferred_element_type=jnp.float32)
        out[0, 0, j] = total.astype(BF)


def product(batch, batches, me, coef, gamma, pos, prior):
    owned = coef.shape[0]
    groups = len(gamma)
    per = 20
    extra = [] if prior is None else [prior]
    return pl.pallas_call(
        functools.partial(product_kernel, per, groups),
        out_shape=[
            jax.ShapeDtypeStruct((batches, 1, owned, BLK, BLK), BF),
            jax.ShapeDtypeStruct((1,), jnp.int32),
        ],
        grid_spec=pltpu.PrefetchScalarGridSpec(
            num_scalar_prefetch=2,
            grid=(owned // per,),
            in_specs=[pl.BlockSpec((per, BLK, coef.shape[2]), lambda i, *_: (i, 0, 0))]
            + [pl.BlockSpec(gamma[0].shape, lambda i, *_: (0, 0, 0))] * groups
            + [ANY] * len(extra),
            out_specs=[
                pl.BlockSpec((1, 1, per, BLK, BLK), lambda i, *_: (batch, 0, i, 0, 0)),
                SMEM,
            ],
            scratch_shapes=[pltpu.VMEM((groups,) + gamma[0].shape, BF)],
        ),
        input_output_aliases={3 + groups: 0} if extra else {},
        compiler_params=params(16),
        cost_estimate=cost(6 << 20, 2 * owned * BLK**3),
        name=f"product{batch}",
    )(me, pos, coef, *gamma, *extra)


def local(gamma_pairs, occ_coef, block_lists, block_counts, block_coords):
    batches, aux, occ, width = gamma_pairs.shape
    groups = lax.axis_size("sp")
    basis = occ_coef.shape[0]
    nblk = basis // BLK
    total_blocks = block_coords.shape[0]
    owned = total_blocks // groups
    capacity = block_lists.shape[2]
    me_s = lax.axis_index("sp")
    me_z = lax.axis_index("z")

    at = jnp.stack([lax.axis_index("x"), lax.axis_index("core")]).astype(jnp.int32)
    pairs = gamma_pairs.reshape(batches, NZ, NX, NCORE, occ, width)

    pairs = pltpu.with_memory_space_constraint(pairs, pltpu.HBM)

    def swap(halves):
        return halves[0], lax.ppermute(halves[1], "core", [(0, 1), (1, 0)])

    split0, block_lists, block_counts, block_coords = lax.optimization_barrier(
        (core_split(0, at, pairs), block_lists, block_counts, block_coords)
    )
    halves0 = swap(split0)

    valid = jnp.arange(capacity, dtype=jnp.int32)[None, None, :] < block_counts[:, :, None]
    lists = jnp.clip(block_lists, 0, owned - 1)
    ids = lists + (jnp.arange(groups, dtype=jnp.int32) * owned)[None, :, None]
    hit = ids.reshape(groups, -1, 1) == jnp.arange(total_blocks, dtype=jnp.int32)
    row_ids = jnp.sum(jnp.where(hit, block_coords[:, 0], 0), axis=2)
    col_ids = jnp.sum(jnp.where(hit, block_coords[:, 1], 0), axis=2)
    live_col = jnp.where(valid.reshape(groups, -1), col_ids, -1)
    need = jnp.any(live_col[:, :, None] == jnp.arange(nblk, dtype=jnp.int32), axis=1)
    pair_blocks = 2 * nblk // (NZ * NX)
    held = -(-2 * width // BLK)
    need = need.reshape(groups, NZ * NX // 2, 1, pair_blocks).astype(jnp.int32)
    need = jnp.concatenate([need[..., :held], need[..., pair_blocks - held :]], axis=2)
    need = need.reshape(groups, NZ * NX, held)
    most = jnp.max(jnp.sum(need, axis=2))
    my_need = lax.dynamic_index_in_dim(need, me_s, 0, keepdims=False)
    tile_ids = jnp.arange(held, dtype=jnp.int32)
    before = (tile_ids[None, :] < tile_ids[:, None]).astype(jnp.int32)
    rank = jnp.sum(my_need[:, None, :] * before[None], axis=2)
    my_cols = lax.dynamic_index_in_dim(col_ids, me_s, 0, keepdims=False)
    my_chip = me_z * NX + lax.axis_index("x")
    chip_need = lax.dynamic_index_in_dim(my_need, my_chip, 0, keepdims=False)
    chip_rank = lax.dynamic_index_in_dim(rank, my_chip, 0, keepdims=False)
    listed = jnp.sum(
        jnp.where(
            (chip_rank[None, :] == tile_ids[:, None]) & (chip_need[None, :] > 0),
            tile_ids[None, :],
            0,
        ),
        axis=1,
    )
    listed = jnp.concatenate([listed, jnp.sum(chip_need, keepdims=True)])
    me = jnp.stack([me_s, me_z]).astype(jnp.int32)

    def exchange_owners(sent):
        return [sent[0]] + [
            lax.ppermute(sent[k], "sp", [(i, (i + k) % groups) for i in range(groups)])
            for k in range(1, groups)
        ]

    def tables(lists, valid, row_ids, my_cols, rank):
        my_live = lax.dynamic_index_in_dim(valid.reshape(groups, -1), me_s, 0, keepdims=False)
        my_rows = lax.dynamic_index_in_dim(row_ids, me_s, 0, keepdims=False)
        slot_cols = my_cols.reshape(groups, capacity)
        slot_cols = jnp.where(my_live.reshape(groups, capacity), slot_cols, slot_cols[:, :1])
        slot_cols = slot_cols.reshape(-1)
        two_chips, within = slot_cols // pair_blocks, slot_cols % pair_blocks
        upper = jnp.arange(2, dtype=jnp.int32)[:, None]
        on_odd = (within[None, :] > held - 1 - upper).astype(jnp.int32)
        chip = 2 * two_chips[None, :] + on_odd
        tile = within[None, :] - on_odd * (pair_blocks - held)
        tile_hit = (chip * held + tile)[:, :, None] == jnp.arange(NZ * NX * held, dtype=jnp.int32)
        order = jnp.sum(jnp.where(tile_hit, rank.reshape(-1), 0), axis=2)
        spots = (8 * chip + order).reshape(-1)
        to_me = lax.dynamic_index_in_dim(lists, me_s, 1, keepdims=False)
        to_me_valid = lax.dynamic_index_in_dim(valid, me_s, 1, keepdims=False)
        hits = (to_me[:, None, :] == jnp.arange(owned, dtype=jnp.int32)[None, :, None]) & to_me_valid[
            :, None, :
        ]
        slot_no = jnp.arange(capacity, dtype=jnp.int32) + 1
        pos = (jnp.sum(jnp.where(hits, slot_no, 0), axis=2) - 1).reshape(-1)

        return my_rows, pos, spots

    def finish(cap, halves0, pairs, coef_t, listed, *lookups):
        def tiles(halves, after):
            halves = [half.reshape(NZ * NX, occ, width) for half in halves]
            picked, token = tile_pick(at, listed, *halves, after, cap)
            return token, lax.all_to_all(picked, ("z", "x"), 0, 0, tiled=True)

        def owners(got, after):
            return exchange_owners(slot_pick(me, spots, got, after, groups))

        token, got0 = tiles(halves0, me)
        *lookups, token = lax.optimization_barrier((*lookups, token))
        my_rows, pos, spots = tables(*lookups)
        coef_parts = exchange_owners(coef_pick(me, coef_t, my_rows, token, groups))
        coef = coef_join(me, coef_parts, pos, owned)
        _, got1 = tiles(swap(core_split(1, at, pairs)), coef)
        out, token = product(0, batches, me, coef, owners(got0, me), pos, None)
        out, _ = product(1, batches, me, coef, owners(got1, token), pos, out)
        return out

    level = sum((most > cap).astype(jnp.int32) for cap in LEVELS[:-1])
    level, listed = lax.optimization_barrier((level, listed))
    lookups = (lists, valid, row_ids, my_cols, rank)
    branches = [functools.partial(finish, cap) for cap in LEVELS]
    return lax.switch(level, branches, halves0, pairs, occ_coef.T, listed, *lookups)


def solution(mesh):
    groups = mesh.shape["sp"]
    grid = Mesh(mesh.devices.reshape(NZ, NX, NCORE, groups), ("z", "x", "core", "sp"))
    pair = ("z", "x", "core")
    in_specs = (P(None, None, "sp", pair), P(None, "sp"), P(), P(), P())
    out_specs = P(None, pair, "sp", None, None)
    return jax.shard_map(local, mesh=grid, in_specs=in_specs, out_specs=out_specs, check_vma=False)
```
